256 devices in a mesh: dp: 4 (over x), expert: 64 (over y, z, core).
Axes of the slice: x: 4, y: 4, z: 8, core: 2. Of those that a mesh axis runs over, the one named last changes fastest.
Arguments:
- tokens: bfloat16 [8192, 2048], P('expert'), may hold values from -4 to 4
- norm_gain: bfloat16 [2048], replicated, may hold values from 0.5 to 1.5
- routing_projection_matrix: bfloat16 [2048, 64], replicated, may hold values from -0.125 to 0.125
- experts: int32 [8192, 8], P('expert'), may hold values from 0 to 63, as said below
- replica_key: int32 [8192, 8], P('expert'), may hold values from 0 to 1048575
- slot_expert: int32 [128], replicated, may hold values from 0 to 63, as said below
- capacity: int32 [128], replicated, may hold values from 4 to 16, as said below
- slot_gate_up_weight: bfloat16 [128, 2048, 2, 1024], P('expert', None, None, 'dp'), may hold values from -0.125 to 0.125
- down_weight: bfloat16 [128, 1024, 2048], P('expert', 'dp'), may hold values from -0.1875 to 0.1875
Outputs:
- mixed: bfloat16 [8192, 2048], P('expert', 'dp')
The draws below stay inside these ranges and needn't reach their ends.
Inputs may be any that keep to these rules, and one draw needn't show every extreme that they name: Each row names 8 different experts. `slot_expert`: every expert occupies at least one slot. `capacity`: for every j the capacities of slots 2 * j and 2 * j + 1 sum to at most 24, and to exactly 24 for some j.
All inputs are finite; a program needn't handle non-finite values.
Results may differ from the reference program's by a relative error of at most 0.012.
Values may be sent and summed in bfloat16 or wider, within the bound.
A program may use at most 128 MiB of HBM per device.

```python
import jax
import jax.numpy as jnp
from jax import lax

D = 2048
FF = 1024
TOP = 8
SPECIALIST_COUNT = 64
SLOT_DEV = 2
SLOTS = 128
UNITS = 256
TOK_DEV = 128
TOKENS = 8192
CAPACITY_HIGH = 16
CAP_LO = 4
CAP_DEV = 24
N_EXPERT = 64


def plan(key):
    device_count = SLOTS // SLOT_DEV
    hot_count = max(SPECIALIST_COUNT // 8, 1)
    order = jax.random.permutation(jax.random.fold_in(key, 11), SPECIALIST_COUNT).astype(jnp.int32)
    hottest = order[:hot_count]
    extra = hottest[jax.random.randint(jax.random.fold_in(key, 12), (SLOTS - SPECIALIST_COUNT,), 0, hot_count)]
    table = jnp.concatenate([order, extra])
    table = table[jax.random.permutation(jax.random.fold_in(key, 13), SLOTS)].astype(jnp.int32)
    first = jax.random.randint(jax.random.fold_in(key, 14), (device_count,), CAP_LO, CAPACITY_HIGH + 1)
    upper = jnp.minimum(CAP_DEV - first, CAPACITY_HIGH)
    second = CAP_LO + jax.random.randint(jax.random.fold_in(key, 15), (device_count,), 0, 1 << 20) % (upper - CAP_LO + 1)
    special = jax.random.randint(jax.random.fold_in(key, 16), (), 0, device_count)
    devices = jnp.arange(device_count)
    first = jnp.where(devices == special, CAPACITY_HIGH, first)
    second = jnp.where(devices == special, CAP_DEV - CAPACITY_HIGH, second)
    lowest = (special + 1) % device_count
    second = jnp.where(devices == lowest, CAP_LO, second)
    capacity = jnp.stack([first, second], axis=1).reshape(SLOTS).astype(jnp.int32)
    selected_specialists = table[2 * special]
    holders = table == selected_specialists
    copies = jnp.sum(holders.astype(jnp.int32))
    before = jnp.sum((holders & (jnp.arange(SLOTS) < 2 * special)).astype(jnp.int32))
    is_hot = jnp.any(jnp.arange(SPECIALIST_COUNT)[:, None] == hottest[None, :], axis=1).astype(jnp.int32)
    minimal_share = jax.random.randint(jax.random.fold_in(key, 17), (TOKENS, SPECIALIST_COUNT), 0, 1 << 16) + (1 << 15) * is_hot[None, :]
    noise = jax.random.randint(jax.random.fold_in(key, 18), (TOKENS // TOK_DEV, TOK_DEV), 0, 1 << 20)
    distinct = noise * TOK_DEV + jnp.arange(TOK_DEV)[None, :]
    ranks = jnp.argsort(jnp.argsort(distinct, axis=1), axis=1)
    pinned_selection = (ranks < CAPACITY_HIGH).reshape(TOKENS)
    leftover_share = (pinned_selection[:, None] & (jnp.arange(SPECIALIST_COUNT)[None, :] == selected_specialists)).astype(jnp.int32) * (1 << 17)
    routing_logit_matrix = (minimal_share + leftover_share) * SPECIALIST_COUNT + jnp.arange(SPECIALIST_COUNT)[None, :]
    _, experts = lax.top_k(routing_logit_matrix, TOP)
    experts = experts.astype(jnp.int32)
    keyed = jax.random.randint(jax.random.fold_in(key, 19), (TOKENS, TOP), 0, 1 << 20)
    steer = pinned_selection[:, None] & (experts == selected_specialists)
    keyed = jnp.where(steer, before + copies * (keyed % 4096), keyed)
    topmost = (ranks.reshape(TOKENS) == TOK_DEV - 1) & (jnp.arange(TOKENS) < TOK_DEV)
    marked = topmost[:, None] & (jnp.arange(TOP)[None, :] == 0)
    keyed = jnp.where(marked, (1 << 20) - 1, keyed).astype(jnp.int32)
    return (table, capacity, experts, keyed)


def draw_experts(key, part):
    return plan(key)[2]


def draw_replica_key(key, part):
    return plan(key)[3]


def draw_slot_expert(key, part):
    return plan(key)[0]


def draw_capacity(key, part):
    return plan(key)[1]


def levels(key, extent, shards, least, high):
    level = 1.0
    for dim, parts in shards:
        steps = jax.random.uniform(jax.random.fold_in(jax.random.fold_in(key, 6), dim), (parts,), jnp.float32, least / len(shards), high / len(shards))
        level = level * jnp.repeat(jnp.exp(steps), extent[dim] // parts).reshape((-1,) + (1,) * (len(extent) - 1 - dim))
    return level


def bell_draw(stream_key, dims, scale, reach, pieces=(), kind=jnp.bfloat16):
    loudness = levels(stream_key, dims, pieces, -0.22, 0.18) if pieces else 1.0
    values = jax.random.normal(stream_key, dims, jnp.float32) * scale * loudness
    return jnp.minimum(jnp.maximum(values, -reach), reach).astype(kind)


def setup_inputs(seed: int = 0) -> dict:
    splits = jax.random.split(jax.random.key(seed), 10)
    return {
        "tokens": bell_draw(splits[0], (TOKENS, D), 0.5, 4.0, ((0, 64),)),
        "norm_gain": jnp.clip(1.0 + 0.1 * jax.random.normal(splits[1], (D,), jnp.float32), 0.5, 1.5).astype(jnp.bfloat16),
        "routing_projection_matrix": bell_draw(splits[2], (D, SPECIALIST_COUNT), D ** -0.5, 0.125),
        "experts": draw_experts(jax.random.fold_in(splits[9], 71), 0),
        "replica_key": draw_replica_key(jax.random.fold_in(splits[9], 71), 0),
        "slot_expert": draw_slot_expert(jax.random.fold_in(splits[9], 71), 0),
        "capacity": draw_capacity(jax.random.fold_in(splits[9], 71), 0),
        "slot_gate_up_weight": bell_draw(splits[7], (SLOTS, D, 2, FF), D ** -0.5, 0.125, ((0, 64), (3, 4))),
        "down_weight": bell_draw(splits[8], (SLOTS, FF, D), FF ** -0.5, 0.1875, ((0, 64), (1, 4))),
    }


def assign_slots(experts, replica_key, slot_expert):
    flat_experts = experts.reshape(-1)
    holders = (flat_experts[:, None] == slot_expert[None, :]).astype(jnp.int32)
    copies = lax.optimization_barrier(jnp.sum(holders, axis=1))
    earlier = jnp.cumsum(holders, axis=1) - holders
    wanted = replica_key.reshape(-1) % copies
    matched = holders * (earlier == wanted[:, None]).astype(jnp.int32)
    numbers = jnp.arange(slot_expert.shape[0], dtype=jnp.int32)
    return lax.optimization_barrier(jnp.sum(matched * numbers[None, :], axis=1)).astype(jnp.int32)

def block_positions(slot_ids):
    onehot = (slot_ids[:, None] == jnp.arange(SLOTS, dtype=jnp.int32)[None, :]).astype(jnp.int32)
    return lax.optimization_barrier(jnp.sum((jnp.cumsum(onehot, axis=0) - onehot) * onehot, axis=1)).astype(jnp.int32)

def reference(tokens, norm_gain, routing_projection_matrix, experts, replica_key, slot_expert, capacity, slot_gate_up_weight, down_weight):
    hidden = tokens.astype(jnp.float32)
    scale = lax.rsqrt(lax.optimization_barrier(jnp.mean(hidden * hidden, axis=-1, keepdims=True)) + 1e-06)
    normed = (hidden * scale * norm_gain.astype(jnp.float32)).astype(jnp.bfloat16)
    logits = jnp.dot(normed, routing_projection_matrix, preferred_element_type=jnp.float32)
    routing_logit_matrix = jax.nn.sigmoid(jnp.take_along_axis(logits, experts, axis=1)).reshape(-1)
    slot_ids = assign_slots(experts, replica_key, slot_expert)
    position = jax.vmap(block_positions)(slot_ids.reshape(N_EXPERT, TOK_DEV * TOP)).reshape(-1)
    kept_mask = position < capacity[slot_ids]
    pair_rows = jnp.arange(TOKENS * TOP, dtype=jnp.int32) // TOP
    blocks = pair_rows // TOK_DEV
    total = SLOTS * N_EXPERT * CAPACITY_HIGH
    target = jnp.where(kept_mask, (slot_ids * N_EXPERT + blocks) * CAPACITY_HIGH + position, total).astype(jnp.int32)
    row_table = jnp.zeros((total + 1,), jnp.int32).at[target].set(pair_rows)[:-1].reshape(SLOTS, N_EXPERT * CAPACITY_HIGH)
    kept_scores = jnp.where(kept_mask, routing_logit_matrix, jnp.float32(0.0))
    weight_table = jnp.zeros((total + 1,), jnp.float32).at[target].set(kept_scores)[:-1].reshape(SLOTS, N_EXPERT * CAPACITY_HIGH)

    def slot_step(mixture, inputs):
        rows, row_weights, gate_up_one, down_one = inputs
        picked = normed[rows]
        gate_up_out = jnp.dot(picked, gate_up_one.reshape(D, 2 * FF), preferred_element_type=jnp.float32)
        activated = (jax.nn.silu(gate_up_out[:, :FF]) * gate_up_out[:, FF:]).astype(jnp.bfloat16)
        result = jnp.zeros((rows.shape[0], D), jnp.float32)
        for section in range(FF // UNITS):
            lower = section * UNITS
            piece = jnp.dot(activated[:, lower:lower + UNITS], down_one[lower:lower + UNITS], preferred_element_type=jnp.float32)
            rounded = lax.optimization_barrier(piece.astype(jnp.bfloat16))
            result = result + rounded.astype(jnp.float32)
        mixture = mixture.at[rows].add(row_weights[:, None] * result)
        return (mixture, None)
    mixture, _ = lax.scan(slot_step, jnp.zeros((TOKENS, D), jnp.float32), (row_table, weight_table, slot_gate_up_weight, down_weight))
    return (hidden + mixture).astype(jnp.bfloat16)
```

```python
import jax
import jax.numpy as jnp
from jax import lax
from jax.sharding import PartitionSpec as P

CAPACITY_HIGH = 16
CAP_DEV = 24


def assign_slots(experts, replica_key, slot_expert):
    flat_experts = experts.reshape(-1)
    holders = (flat_experts[:, None] == slot_expert[None, :]).astype(jnp.int32)
    copies = jnp.sum(holders, axis=1)
    earlier = jnp.cumsum(holders, axis=1) - holders
    wanted = replica_key.reshape(-1) % copies
    matched = holders * (earlier == wanted[:, None]).astype(jnp.int32)
    numbers = jnp.arange(slot_expert.shape[0], dtype=jnp.int32)
    return jnp.sum(matched * numbers[None, :], axis=1)


def slot_partial(flat_rows, gate_up_one, down_one):
    model_width = flat_rows.shape[1]
    unit_count = gate_up_one.shape[2]
    gate_up_out = jnp.dot(
        flat_rows,
        gate_up_one.reshape(model_width, 2 * unit_count),
        preferred_element_type=jnp.float32,
    )
    activated = (jax.nn.silu(gate_up_out[:, :unit_count]) * gate_up_out[:, unit_count:]).astype(
        jnp.bfloat16
    )
    result = jnp.dot(activated, down_one, preferred_element_type=jnp.float32)
    return result.astype(jnp.bfloat16)


def on_device(
    tokens,
    norm_gain,
    routing_projection_matrix,
    experts,
    replica_key,
    slot_expert,
    capacity,
    slot_gate_up_weight,
    down_weight,
):
    peer_count = lax.axis_size("expert")
    group_count = lax.axis_size("dp")
    group_pos = lax.axis_index("dp")
    me = lax.axis_index("expert")
    rows_here = tokens.shape[0]
    model_width = tokens.shape[1]
    pick_count = experts.shape[1]
    slot_count = slot_expert.shape[0]
    per_device = slot_count // peer_count
    quarter = model_width // group_count
    buffer_rows = CAP_DEV

    hidden = tokens.astype(jnp.float32)
    scale = lax.rsqrt(jnp.mean(hidden * hidden, axis=-1, keepdims=True) + 1e-06)
    normed = (hidden * scale * norm_gain.astype(jnp.float32)).astype(jnp.bfloat16)
    logits = jnp.dot(normed, routing_projection_matrix, preferred_element_type=jnp.float32)
    score = jax.nn.sigmoid(jnp.take_along_axis(logits, experts, axis=1)).reshape(-1)

    slot_ids = assign_slots(experts, replica_key, slot_expert)
    onehot = (slot_ids[:, None] == jnp.arange(slot_count, dtype=jnp.int32)[None, :]).astype(
        jnp.int32
    )
    position = jnp.sum((jnp.cumsum(onehot, axis=0) - onehot) * onehot, axis=1)
    slot_cap = jnp.sum(onehot * capacity[None, :], axis=1)
    kept_mask = position < slot_cap
    is_second = (slot_ids % per_device) == 1
    row_in = jnp.where(is_second, buffer_rows - slot_cap + position, position)
    target = jnp.where(
        kept_mask, slot_ids // per_device * buffer_rows + row_in, peer_count * buffer_rows
    )
    source_rows = jnp.arange(rows_here * pick_count, dtype=jnp.int32) // pick_count

    normed_part = lax.dynamic_slice_in_dim(normed, group_pos * quarter, quarter, 1)
    outgoing = (
        jnp.zeros((peer_count * buffer_rows + 1, quarter), jnp.bfloat16)
        .at[target]
        .set(normed_part[source_rows])
    )
    outgoing = outgoing[:-1].reshape(peer_count, buffer_rows, quarter)
    incoming_part = lax.all_to_all(outgoing, "expert", split_axis=0, concat_axis=0, tiled=True)
    incoming = lax.all_gather(incoming_part, "dp", axis=2, tiled=True)
    flat_in = incoming.reshape(peer_count * buffer_rows, model_width)

    first_out = slot_partial(flat_in, slot_gate_up_weight[0], down_weight[0])
    second_out = slot_partial(flat_in, slot_gate_up_weight[1], down_weight[1])
    first_cap = lax.dynamic_index_in_dim(capacity, me * per_device, keepdims=False)
    row_index = jnp.arange(peer_count * buffer_rows, dtype=jnp.int32) % buffer_rows
    partial_value = jnp.where((row_index < first_cap)[:, None], first_out, second_out)
    partial_value = partial_value.reshape(peer_count, buffer_rows, model_width)

    summed = lax.psum_scatter(partial_value, "dp", scatter_dimension=2, tiled=True)
    returned = lax.all_to_all(summed, "expert", split_axis=0, concat_axis=0, tiled=True)

    flat_ret = returned.reshape(peer_count * buffer_rows, quarter)
    flat_ret = jnp.concatenate([flat_ret, jnp.zeros((1, quarter), flat_ret.dtype)])
    weight_kept = jnp.where(kept_mask, score, jnp.float32(0.0))
    gathered = flat_ret[target].astype(jnp.float32).reshape(rows_here, pick_count, quarter)
    mixture = jnp.sum(weight_kept.reshape(rows_here, pick_count)[:, :, None] * gathered, axis=1)
    residual = lax.dynamic_slice_in_dim(tokens, group_pos * quarter, quarter, 1).astype(jnp.float32)
    return (residual + mixture).astype(jnp.bfloat16)


def solution(mesh):
    in_specs = (
        P("expert", None),
        P(),
        P(),
        P("expert", None),
        P("expert", None),
        P(),
        P(),
        P("expert", None, None, "dp"),
        P("expert", "dp", None),
    )
    out_specs = P("expert", "dp")
    return jax.shard_map(
        on_device, mesh=mesh, in_specs=in_specs, out_specs=out_specs, check_vma=False
    )
```

```python
import jax
import jax.numpy as jnp
from jax import lax
from jax.sharding import PartitionSpec as P

CAPACITY_HIGH = 16
CAP_DEV = 24


def assign_slots(experts, replica_key, slot_expert):
    flat_experts = experts.reshape(-1)
    holders = (flat_experts[:, None] == slot_expert[None, :]).astype(jnp.int32)
    copies = jnp.sum(holders, axis=1)
    earlier = jnp.cumsum(holders, axis=1) - holders
    wanted = replica_key.reshape(-1) % copies
    matched = holders * (earlier == wanted[:, None]).astype(jnp.int32)
    numbers = jnp.arange(slot_expert.shape[0], dtype=jnp.int32)
    return jnp.sum(matched * numbers[None, :], axis=1)


def slot_activated(flat_rows, gate_up_one):
    model_width = flat_rows.shape[1]
    unit_count = gate_up_one.shape[2]
    gate_up_out = jnp.dot(
        flat_rows,
        gate_up_one.reshape(model_width, 2 * unit_count),
        preferred_element_type=jnp.float32,
    )
    return (jax.nn.silu(gate_up_out[:, :unit_count]) * gate_up_out[:, unit_count:]).astype(
        jnp.bfloat16
    )


def group_sums(act_all, down_cols, unit_count):
    total = None
    for lower in range(0, act_all.shape[1], unit_count):
        piece = jnp.dot(
            act_all[:, lower:lower + unit_count],
            down_cols[lower:lower + unit_count],
            preferred_element_type=jnp.float32,
        )
        piece = piece.astype(jnp.bfloat16).astype(jnp.float32)
        total = piece if total is None else total + piece
    return total


def on_device(
    tokens,
    norm_gain,
    routing_projection_matrix,
    experts,
    replica_key,
    slot_expert,
    capacity,
    slot_gate_up_weight,
    down_weight,
):
    peer_count = lax.axis_size("expert")
    group_count = lax.axis_size("dp")
    group_pos = lax.axis_index("dp")
    me = lax.axis_index("expert")
    rows_here = tokens.shape[0]
    model_width = tokens.shape[1]
    pick_count = experts.shape[1]
    slot_count = slot_expert.shape[0]
    per_device = slot_count // peer_count
    quarter = model_width // group_count
    buffer_rows = CAP_DEV

    hidden = tokens.astype(jnp.float32)
    scale = lax.rsqrt(jnp.mean(hidden * hidden, axis=-1, keepdims=True) + 1e-06)
    normed = (hidden * scale * norm_gain.astype(jnp.float32)).astype(jnp.bfloat16)
    logits = jnp.dot(normed, routing_projection_matrix, preferred_element_type=jnp.float32)
    score = jax.nn.sigmoid(jnp.take_along_axis(logits, experts, axis=1)).reshape(-1)

    slot_ids = assign_slots(experts, replica_key, slot_expert)
    onehot = (slot_ids[:, None] == jnp.arange(slot_count, dtype=jnp.int32)[None, :]).astype(
        jnp.int32
    )
    position = jnp.sum((jnp.cumsum(onehot, axis=0) - onehot) * onehot, axis=1)
    slot_cap = jnp.sum(onehot * capacity[None, :], axis=1)
    kept_mask = position < slot_cap
    is_second = (slot_ids % per_device) == 1
    row_in = jnp.where(is_second, buffer_rows - slot_cap + position, position)
    target = jnp.where(
        kept_mask, slot_ids // per_device * buffer_rows + row_in, peer_count * buffer_rows
    )
    source_rows = jnp.arange(rows_here * pick_count, dtype=jnp.int32) // pick_count

    normed_part = lax.dynamic_slice_in_dim(normed, group_pos * quarter, quarter, 1)
    outgoing = (
        jnp.zeros((peer_count * buffer_rows + 1, quarter), jnp.bfloat16)
        .at[target]
        .set(normed_part[source_rows])
    )
    outgoing = outgoing[:-1].reshape(peer_count, buffer_rows, quarter)
    incoming_part = lax.all_to_all(outgoing, "expert", split_axis=0, concat_axis=0, tiled=True)
    incoming = lax.all_gather(incoming_part, "dp", axis=2, tiled=True)
    flat_in = incoming.reshape(peer_count * buffer_rows, model_width)

    first_act = slot_activated(flat_in, slot_gate_up_weight[0])
    second_act = slot_activated(flat_in, slot_gate_up_weight[1])
    first_cap = lax.dynamic_index_in_dim(capacity, me * per_device, keepdims=False)
    row_index = jnp.arange(peer_count * buffer_rows, dtype=jnp.int32) % buffer_rows
    in_first = (row_index < first_cap)[:, None]
    act_here = jnp.where(in_first, first_act, second_act)
    act_all = lax.all_gather(act_here, "dp", axis=1, tiled=True)
    down_here = lax.all_to_all(down_weight, "dp", split_axis=2, concat_axis=1, tiled=True)
    unit_count = down_weight.shape[1]
    first_sum = group_sums(act_all, down_here[0], unit_count)
    second_sum = group_sums(act_all, down_here[1], unit_count)
    expert_out = jnp.where(in_first, first_sum, second_sum).astype(jnp.bfloat16)
    summed = expert_out.reshape(peer_count, buffer_rows, quarter)
    returned = lax.all_to_all(summed, "expert", split_axis=0, concat_axis=0, tiled=True)

    flat_ret = returned.reshape(peer_count * buffer_rows, quarter)
    flat_ret = jnp.concatenate([flat_ret, jnp.zeros((1, quarter), flat_ret.dtype)])
    weight_kept = jnp.where(kept_mask, score, jnp.float32(0.0))
    gathered = flat_ret[target].astype(jnp.float32).reshape(rows_here, pick_count, quarter)
    mixture = jnp.sum(weight_kept.reshape(rows_here, pick_count)[:, :, None] * gathered, axis=1)
    residual = lax.dynamic_slice_in_dim(tokens, group_pos * quarter, quarter, 1).astype(jnp.float32)
    return (residual + mixture).astype(jnp.bfloat16)


def solution(mesh):
    in_specs = (
        P("expert", None),
        P(),
        P(),
        P("expert", None),
        P("expert", None),
        P(),
        P(),
        P("expert", None, None, "dp"),
        P("expert", "dp", None),
    )
    out_specs = P("expert", "dp")
    return jax.shard_map(
        on_device, mesh=mesh, in_specs=in_specs, out_specs=out_specs, check_vma=False
    )
```

```python
import functools

import jax
import jax.numpy as jnp
from jax import lax
from jax.experimental import pallas as pl
from jax.experimental.pallas import tpu as pltpu
from jax.sharding import PartitionSpec as P

MESH = pl.DeviceIdType.MESH

CAPACITY_HIGH = 16
CAP_DEV = 24


def exchange_kernel(n_exp, n_dp, with_down, *refs):
    if with_down:
        send_ref, down_ref, recv_ref, down_out, a_send, a_recv, d_send, d_recv, local_sem = refs
    else:
        send_ref, recv_ref, a_send, a_recv, local_sem = refs
    me = lax.axis_index("expert")
    gi = lax.axis_index("dp")

    def a2a_copy(j, recv_slot):
        return pltpu.make_async_remote_copy(
            src_ref=send_ref.at[j],
            dst_ref=recv_ref.at[recv_slot],
            send_sem=a_send.at[j],
            recv_sem=a_recv.at[recv_slot],
            device_id=(gi, j),
            device_id_type=MESH,
        )

    def down_copy(g, recv_slot):
        q = down_out.shape[-1]
        cols = pl.ds(pl.multiple_of(g * q, 128), q)
        return pltpu.make_async_remote_copy(
            src_ref=down_ref.at[:, :, cols],
            dst_ref=down_out.at[recv_slot],
            send_sem=d_send.at[g],
            recv_sem=d_recv.at[recv_slot],
            device_id=(g, me),
            device_id_type=MESH,
        )

    barrier = pltpu.get_barrier_semaphore()

    def greet(k, carry):
        j = lax.rem(me + k, n_exp)
        pl.semaphore_signal(barrier, 1, device_id=(gi, j), device_id_type=MESH)
        return carry

    lax.fori_loop(1, n_exp, greet, 0)
    greet_count = n_exp - 1
    if with_down:
        for k in range(1, n_dp):
            g = lax.rem(gi + k, n_dp)
            pl.semaphore_signal(barrier, 1, device_id=(g, me), device_id_type=MESH)
        greet_count += n_dp - 1
    pl.semaphore_wait(barrier, greet_count)

    def send_one(k, carry):
        j = lax.rem(me + k, n_exp)
        a2a_copy(j, me).start()
        return carry

    lax.fori_loop(1, n_exp, send_one, 0)
    local = pltpu.make_async_copy(send_ref.at[me], recv_ref.at[me], local_sem.at[0])
    local.start()
    if with_down:
        q = down_out.shape[-1]
        for k in range(1, n_dp):
            down_copy(lax.rem(gi + k, n_dp), gi).start()
        own_cols = pl.ds(pl.multiple_of(gi * q, 128), q)
        local_down = pltpu.make_async_copy(
            down_ref.at[:, :, own_cols], down_out.at[gi], local_sem.at[1]
        )
        local_down.start()

    def wait_one(k, carry):
        j = lax.rem(me + k, n_exp)
        a2a_copy(j, me).wait_send()
        a2a_copy(j, j).wait_recv()
        return carry

    lax.fori_loop(1, n_exp, wait_one, 0)
    local.wait()
    if with_down:
        for k in range(1, n_dp):
            g = lax.rem(gi + k, n_dp)
            down_copy(g, gi).wait_send()
            down_copy(g, g).wait_recv()
        local_down.wait()


def exchange(send, down=None, collective_id=0):
    n_exp = lax.axis_size("expert")
    n_dp = lax.axis_size("dp")
    with_down = down is not None
    any_spec = pl.BlockSpec(memory_space=pl.ANY)
    out_shape = [jax.ShapeDtypeStruct(send.shape, send.dtype)]
    scratch = [pltpu.SemaphoreType.DMA((n_exp,)), pltpu.SemaphoreType.DMA((n_exp,))]
    operands = [send]
    moved = send.size * send.dtype.itemsize
    if with_down:
        q = down.shape[-1] // n_dp
        out_shape.append(jax.ShapeDtypeStruct((n_dp,) + down.shape[:-1] + (q,), down.dtype))
        scratch += [pltpu.SemaphoreType.DMA((n_dp,)), pltpu.SemaphoreType.DMA((n_dp,))]
        operands.append(down)
        moved += down.size * down.dtype.itemsize
    scratch.append(pltpu.SemaphoreType.DMA((2,)))
    return pl.pallas_call(
        functools.partial(exchange_kernel, n_exp, n_dp, with_down),
        out_shape=tuple(out_shape),
        in_specs=[any_spec] * len(operands),
        out_specs=tuple([any_spec] * len(out_shape)),
        scratch_shapes=scratch,
        compiler_params=pltpu.CompilerParams(collective_id=collective_id, has_side_effects=True),
        cost_estimate=pl.CostEstimate(flops=0, transcendentals=0, bytes_accessed=2 * moved),
    )(*operands)


def assign_slots(experts, replica_key, slot_expert):
    flat_experts = experts.reshape(-1)
    holders = (flat_experts[:, None] == slot_expert[None, :]).astype(jnp.int32)
    copies = jnp.sum(holders, axis=1)
    earlier = jnp.cumsum(holders, axis=1) - holders
    wanted = replica_key.reshape(-1) % copies
    matched = holders * (earlier == wanted[:, None]).astype(jnp.int32)
    numbers = jnp.arange(slot_expert.shape[0], dtype=jnp.int32)
    return jnp.sum(matched * numbers[None, :], axis=1)


def slot_activated(flat_rows, gate_up_one):
    model_width = flat_rows.shape[1]
    unit_count = gate_up_one.shape[2]
    gate_up_out = jnp.dot(
        flat_rows,
        gate_up_one.reshape(model_width, 2 * unit_count),
        preferred_element_type=jnp.float32,
    )
    return (jax.nn.silu(gate_up_out[:, :unit_count]) * gate_up_out[:, unit_count:]).astype(
        jnp.bfloat16
    )


def group_sums(act_all, down_cols, unit_count):
    total = None
    for lower in range(0, act_all.shape[1], unit_count):
        piece = jnp.dot(
            act_all[:, lower:lower + unit_count],
            down_cols[lower:lower + unit_count],
            preferred_element_type=jnp.float32,
        )
        piece = piece.astype(jnp.bfloat16).astype(jnp.float32)
        total = piece if total is None else total + piece
    return total


def on_device(
    tokens,
    norm_gain,
    routing_projection_matrix,
    experts,
    replica_key,
    slot_expert,
    capacity,
    slot_gate_up_weight,
    down_weight,
):
    peer_count = lax.axis_size("expert")
    group_count = lax.axis_size("dp")
    group_pos = lax.axis_index("dp")
    me = lax.axis_index("expert")
    rows_here = tokens.shape[0]
    model_width = tokens.shape[1]
    pick_count = experts.shape[1]
    slot_count = slot_expert.shape[0]
    per_device = slot_count // peer_count
    quarter = model_width // group_count
    buffer_rows = CAP_DEV

    hidden = tokens.astype(jnp.float32)
    scale = lax.rsqrt(jnp.mean(hidden * hidden, axis=-1, keepdims=True) + 1e-06)
    normed = (hidden * scale * norm_gain.astype(jnp.float32)).astype(jnp.bfloat16)
    logits = jnp.dot(normed, routing_projection_matrix, preferred_element_type=jnp.float32)
    score = jax.nn.sigmoid(jnp.take_along_axis(logits, experts, axis=1)).reshape(-1)

    slot_ids = assign_slots(experts, replica_key, slot_expert)
    onehot = (slot_ids[:, None] == jnp.arange(slot_count, dtype=jnp.int32)[None, :]).astype(
        jnp.int32
    )
    position = jnp.sum((jnp.cumsum(onehot, axis=0) - onehot) * onehot, axis=1)
    slot_cap = jnp.sum(onehot * capacity[None, :], axis=1)
    kept_mask = position < slot_cap
    is_second = (slot_ids % per_device) == 1
    row_in = jnp.where(is_second, buffer_rows - slot_cap + position, position)
    target = jnp.where(
        kept_mask, slot_ids // per_device * buffer_rows + row_in, peer_count * buffer_rows
    )
    source_rows = jnp.arange(rows_here * pick_count, dtype=jnp.int32) // pick_count

    normed_part = lax.dynamic_slice_in_dim(normed, group_pos * quarter, quarter, 1)
    outgoing = (
        jnp.zeros((peer_count * buffer_rows + 1, quarter), jnp.bfloat16)
        .at[target]
        .set(normed_part[source_rows])
    )
    outgoing = outgoing[:-1].reshape(peer_count, buffer_rows, quarter)
    incoming_part, down_parts = exchange(outgoing, down_weight, collective_id=0)
    incoming = lax.all_gather(incoming_part, "dp", axis=2, tiled=True)
    flat_in = incoming.reshape(peer_count * buffer_rows, model_width)

    first_act = slot_activated(flat_in, slot_gate_up_weight[0])
    second_act = slot_activated(flat_in, slot_gate_up_weight[1])
    first_cap = lax.dynamic_index_in_dim(capacity, me * per_device, keepdims=False)
    row_index = jnp.arange(peer_count * buffer_rows, dtype=jnp.int32) % buffer_rows
    in_first = (row_index < first_cap)[:, None]
    act_here = jnp.where(in_first, first_act, second_act)
    act_all = lax.all_gather(act_here, "dp", axis=1, tiled=True)
    down_here = jnp.swapaxes(down_parts, 0, 1).reshape(per_device, -1, quarter)
    unit_count = down_weight.shape[1]
    first_sum = group_sums(act_all, down_here[0], unit_count)
    second_sum = group_sums(act_all, down_here[1], unit_count)
    expert_out = jnp.where(in_first, first_sum, second_sum).astype(jnp.bfloat16)
    summed = expert_out.reshape(peer_count, buffer_rows, quarter)
    (returned,) = exchange(summed, collective_id=1)

    flat_ret = returned.reshape(peer_count * buffer_rows, quarter)
    flat_ret = jnp.concatenate([flat_ret, jnp.zeros((1, quarter), flat_ret.dtype)])
    weight_kept = jnp.where(kept_mask, score, jnp.float32(0.0))
    gathered = flat_ret[target].astype(jnp.float32).reshape(rows_here, pick_count, quarter)
    mixture = jnp.sum(weight_kept.reshape(rows_here, pick_count)[:, :, None] * gathered, axis=1)
    residual = lax.dynamic_slice_in_dim(tokens, group_pos * quarter, quarter, 1).astype(jnp.float32)
    return (residual + mixture).astype(jnp.bfloat16)


def solution(mesh):
    in_specs = (
        P("expert", None),
        P(),
        P(),
        P("expert", None),
        P("expert", None),
        P(),
        P(),
        P("expert", None, None, "dp"),
        P("expert", "dp", None),
    )
    out_specs = P("expert", "dp")
    return jax.shard_map(
        on_device, mesh=mesh, in_specs=in_specs, out_specs=out_specs, check_vma=False
    )
```

```python
import functools

import jax
import jax.numpy as jnp
from jax import lax
from jax.experimental import pallas as pl
from jax.experimental.pallas import tpu as pltpu
from jax.sharding import PartitionSpec as P

MESH = pl.DeviceIdType.MESH

CAPACITY_HIGH = 16
CAP_DEV = 24


def exchange_kernel(n_exp, n_dp, with_down, *refs):
    if with_down:
        send_ref, down_ref, recv_ref, down_out, a_send, a_recv, d_send, d_recv, local_sem = refs
    else:
        send_ref, recv_ref, a_send, a_recv, local_sem = refs
    me = lax.axis_index("expert")
    gi = lax.axis_index("dp")

    def a2a_copy(j, recv_slot):
        return pltpu.make_async_remote_copy(
            src_ref=send_ref.at[j],
            dst_ref=recv_ref.at[recv_slot],
            send_sem=a_send.at[j],
            recv_sem=a_recv.at[recv_slot],
            device_id=(gi, j),
            device_id_type=MESH,
        )

    def down_copy(g, recv_slot):
        q = down_out.shape[-1]
        cols = pl.ds(pl.multiple_of(g * q, 128), q)
        return pltpu.make_async_remote_copy(
            src_ref=down_ref.at[:, :, cols],
            dst_ref=down_out.at[recv_slot],
            send_sem=d_send.at[g],
            recv_sem=d_recv.at[recv_slot],
            device_id=(g, me),
            device_id_type=MESH,
        )

    barrier = pltpu.get_barrier_semaphore()

    def greet(k, carry):
        j = lax.rem(me + k, n_exp)
        pl.semaphore_signal(barrier, 1, device_id=(gi, j), device_id_type=MESH)
        return carry

    lax.fori_loop(1, n_exp, greet, 0)
    greet_count = n_exp - 1
    if with_down:
        for k in range(1, n_dp):
            g = lax.rem(gi + k, n_dp)
            pl.semaphore_signal(barrier, 1, device_id=(g, me), device_id_type=MESH)
        greet_count += n_dp - 1
    pl.semaphore_wait(barrier, greet_count)

    def send_one(k, carry):
        j = lax.rem(me + k, n_exp)
        a2a_copy(j, me).start()
        return carry

    lax.fori_loop(1, n_exp, send_one, 0)
    local = pltpu.make_async_copy(send_ref.at[me], recv_ref.at[me], local_sem.at[0])
    local.start()
    if with_down:
        q = down_out.shape[-1]
        for k in range(1, n_dp):
            down_copy(lax.rem(gi + k, n_dp), gi).start()
        own_cols = pl.ds(pl.multiple_of(gi * q, 128), q)
        local_down = pltpu.make_async_copy(
            down_ref.at[:, :, own_cols], down_out.at[gi], local_sem.at[1]
        )
        local_down.start()

    def wait_one(k, carry):
        j = lax.rem(me + k, n_exp)
        a2a_copy(j, me).wait_send()
        a2a_copy(j, j).wait_recv()
        return carry

    lax.fori_loop(1, n_exp, wait_one, 0)
    local.wait()
    if with_down:
        for k in range(1, n_dp):
            g = lax.rem(gi + k, n_dp)
            down_copy(g, gi).wait_send()
            down_copy(g, g).wait_recv()
        local_down.wait()


def exchange(send, down=None, collective_id=0):
    n_exp = lax.axis_size("expert")
    n_dp = lax.axis_size("dp")
    with_down = down is not None
    any_spec = pl.BlockSpec(memory_space=pl.ANY)
    out_shape = [jax.ShapeDtypeStruct(send.shape, send.dtype)]
    scratch = [pltpu.SemaphoreType.DMA((n_exp,)), pltpu.SemaphoreType.DMA((n_exp,))]
    operands = [send]
    moved = send.size * send.dtype.itemsize
    if with_down:
        q = down.shape[-1] // n_dp
        out_shape.append(jax.ShapeDtypeStruct((n_dp,) + down.shape[:-1] + (q,), down.dtype))
        scratch += [pltpu.SemaphoreType.DMA((n_dp,)), pltpu.SemaphoreType.DMA((n_dp,))]
        operands.append(down)
        moved += down.size * down.dtype.itemsize
    scratch.append(pltpu.SemaphoreType.DMA((2,)))
    return pl.pallas_call(
        functools.partial(exchange_kernel, n_exp, n_dp, with_down),
        out_shape=tuple(out_shape),
        in_specs=[any_spec] * len(operands),
        out_specs=tuple([any_spec] * len(out_shape)),
        scratch_shapes=scratch,
        compiler_params=pltpu.CompilerParams(collective_id=collective_id, has_side_effects=True),
        cost_estimate=pl.CostEstimate(flops=0, transcendentals=0, bytes_accessed=2 * moved),
    )(*operands)


def dispatch_kernel(n_exp, n_dp, send_ref, down_ref, full_ref, down_out,
                    a_send, a_recv, d_send, d_recv, f_send, f_recv, local_sem):
    me = lax.axis_index("expert")
    gi = lax.axis_index("dp")
    q = down_out.shape[-1]

    def a2a_copy(j, recv_slot):
        return pltpu.make_async_remote_copy(
            src_ref=send_ref.at[j],
            dst_ref=full_ref.at[gi, recv_slot],
            send_sem=a_send.at[j],
            recv_sem=a_recv.at[recv_slot],
            device_id=(gi, j),
            device_id_type=MESH,
        )

    def down_copy(g, recv_slot):
        cols = pl.ds(pl.multiple_of(g * q, 128), q)
        return pltpu.make_async_remote_copy(
            src_ref=down_ref.at[:, :, cols],
            dst_ref=down_out.at[recv_slot],
            send_sem=d_send.at[g],
            recv_sem=d_recv.at[recv_slot],
            device_id=(g, me),
            device_id_type=MESH,
        )

    def forward_copy(g, piece):
        return pltpu.make_async_remote_copy(
            src_ref=full_ref.at[gi, piece],
            dst_ref=full_ref.at[gi, piece],
            send_sem=f_send.at[g],
            recv_sem=f_recv.at[gi],
            device_id=(g, me),
            device_id_type=MESH,
        )

    def whole_from(g):
        return pltpu.make_async_remote_copy(
            src_ref=full_ref.at[gi],
            dst_ref=full_ref.at[g],
            send_sem=f_send.at[g],
            recv_sem=f_recv.at[g],
            device_id=(g, me),
            device_id_type=MESH,
        )

    barrier = pltpu.get_barrier_semaphore()

    def greet(k, carry):
        j = lax.rem(me + k, n_exp)
        pl.semaphore_signal(barrier, 1, device_id=(gi, j), device_id_type=MESH)
        return carry

    lax.fori_loop(1, n_exp, greet, 0)
    for k in range(1, n_dp):
        g = lax.rem(gi + k, n_dp)
        pl.semaphore_signal(barrier, 1, device_id=(g, me), device_id_type=MESH)
    pl.semaphore_wait(barrier, n_exp - 1 + n_dp - 1)

    def send_one(k, carry):
        a2a_copy(lax.rem(me + k, n_exp), me).start()
        return carry

    lax.fori_loop(1, n_exp, send_one, 0)
    local = pltpu.make_async_copy(send_ref.at[me], full_ref.at[gi, me], local_sem.at[0])
    local.start()
    for k in range(1, n_dp):
        down_copy(lax.rem(gi + k, n_dp), gi).start()
    own_cols = pl.ds(pl.multiple_of(gi * q, 128), q)
    local_down = pltpu.make_async_copy(down_ref.at[:, :, own_cols], down_out.at[gi], local_sem.at[1])
    local_down.start()

    local.wait()
    for k in range(1, n_dp):
        forward_copy(lax.rem(gi + k, n_dp), me).start()

    def take_one(k, carry):
        j = lax.rem(me - k + n_exp, n_exp)
        a2a_copy(j, j).wait_recv()
        for step in range(1, n_dp):
            forward_copy(lax.rem(gi + step, n_dp), j).start()
        return carry

    lax.fori_loop(1, n_exp, take_one, 0)

    def sent_one(k, carry):
        a2a_copy(lax.rem(me + k, n_exp), me).wait_send()
        return carry

    lax.fori_loop(1, n_exp, sent_one, 0)
    for k in range(1, n_dp):
        g = lax.rem(gi + k, n_dp)
        down_copy(g, gi).wait_send()
        down_copy(g, g).wait_recv()
        whole_from(g).wait_send()
        whole_from(g).wait_recv()
    local_down.wait()


def dispatch(send, down):
    n_exp = lax.axis_size("expert")
    n_dp = lax.axis_size("dp")
    q = down.shape[-1] // n_dp
    any_spec = pl.BlockSpec(memory_space=pl.ANY)
    moved = send.size * send.dtype.itemsize * n_dp + down.size * down.dtype.itemsize
    return pl.pallas_call(
        functools.partial(dispatch_kernel, n_exp, n_dp),
        out_shape=(
            jax.ShapeDtypeStruct((n_dp,) + send.shape, send.dtype),
            jax.ShapeDtypeStruct((n_dp,) + down.shape[:-1] + (q,), down.dtype),
        ),
        in_specs=[any_spec, any_spec],
        out_specs=(any_spec, any_spec),
        scratch_shapes=[
            pltpu.SemaphoreType.DMA((n_exp,)),
            pltpu.SemaphoreType.DMA((n_exp,)),
            pltpu.SemaphoreType.DMA((n_dp,)),
            pltpu.SemaphoreType.DMA((n_dp,)),
            pltpu.SemaphoreType.DMA((n_dp,)),
            pltpu.SemaphoreType.DMA((n_dp,)),
            pltpu.SemaphoreType.DMA((2,)),
        ],
        compiler_params=pltpu.CompilerParams(collective_id=2, has_side_effects=True),
        cost_estimate=pl.CostEstimate(flops=0, transcendentals=0, bytes_accessed=2 * moved),
    )(send, down)


def assign_slots(experts, replica_key, slot_expert):
    flat_experts = experts.reshape(-1)
    holders = (flat_experts[:, None] == slot_expert[None, :]).astype(jnp.int32)
    copies = jnp.sum(holders, axis=1)
    earlier = jnp.cumsum(holders, axis=1) - holders
    wanted = replica_key.reshape(-1) % copies
    matched = holders * (earlier == wanted[:, None]).astype(jnp.int32)
    numbers = jnp.arange(slot_expert.shape[0], dtype=jnp.int32)
    return jnp.sum(matched * numbers[None, :], axis=1)


def slot_activated(quarters, gate_up_one):
    group_count, _, quarter = quarters.shape
    unit_count = gate_up_one.shape[2]
    gate_up_out = lax.dot_general(
        quarters,
        gate_up_one.reshape(group_count, quarter, 2 * unit_count),
        (((0, 2), (0, 1)), ((), ())),
        preferred_element_type=jnp.float32,
    )
    return (jax.nn.silu(gate_up_out[:, :unit_count]) * gate_up_out[:, unit_count:]).astype(
        jnp.bfloat16
    )


def group_sums(act_all, down_cols, unit_count):
    total = None
    for lower in range(0, act_all.shape[1], unit_count):
        piece = jnp.dot(
            act_all[:, lower:lower + unit_count],
            down_cols[lower:lower + unit_count],
            preferred_element_type=jnp.float32,
        )
        piece = piece.astype(jnp.bfloat16).astype(jnp.float32)
        total = piece if total is None else total + piece
    return total


def on_device(
    tokens,
    norm_gain,
    routing_projection_matrix,
    experts,
    replica_key,
    slot_expert,
    capacity,
    slot_gate_up_weight,
    down_weight,
):
    peer_count = lax.axis_size("expert")
    group_count = lax.axis_size("dp")
    group_pos = lax.axis_index("dp")
    me = lax.axis_index("expert")
    rows_here = tokens.shape[0]
    model_width = tokens.shape[1]
    pick_count = experts.shape[1]
    slot_count = slot_expert.shape[0]
    per_device = slot_count // peer_count
    quarter = model_width // group_count
    buffer_rows = CAP_DEV

    hidden = tokens.astype(jnp.float32)
    scale = lax.rsqrt(jnp.mean(hidden * hidden, axis=-1, keepdims=True) + 1e-06)
    normed = (hidden * scale * norm_gain.astype(jnp.float32)).astype(jnp.bfloat16)
    logits = jnp.dot(normed, routing_projection_matrix, preferred_element_type=jnp.float32)
    score = jax.nn.sigmoid(jnp.take_along_axis(logits, experts, axis=1)).reshape(-1)

    slot_ids = assign_slots(experts, replica_key, slot_expert)
    onehot = (slot_ids[:, None] == jnp.arange(slot_count, dtype=jnp.int32)[None, :]).astype(
        jnp.int32
    )
    position = jnp.sum((jnp.cumsum(onehot, axis=0) - onehot) * onehot, axis=1)
    slot_cap = jnp.sum(onehot * capacity[None, :], axis=1)
    kept_mask = position < slot_cap
    is_second = (slot_ids % per_device) == 1
    row_in = jnp.where(is_second, buffer_rows - slot_cap + position, position)
    target = jnp.where(
        kept_mask, slot_ids // per_device * buffer_rows + row_in, peer_count * buffer_rows
    )
    source_rows = jnp.arange(rows_here * pick_count, dtype=jnp.int32) // pick_count

    normed_part = lax.dynamic_slice_in_dim(normed, group_pos * quarter, quarter, 1)
    outgoing = (
        jnp.zeros((peer_count * buffer_rows + 1, quarter), jnp.bfloat16)
        .at[target]
        .set(normed_part[source_rows])
    )
    outgoing = outgoing[:-1].reshape(peer_count, buffer_rows, quarter)
    full_in, down_parts = dispatch(outgoing, down_weight)
    quarters = full_in.reshape(group_count, peer_count * buffer_rows, quarter)

    first_act = slot_activated(quarters, slot_gate_up_weight[0])
    second_act = slot_activated(quarters, slot_gate_up_weight[1])
    first_cap = lax.dynamic_index_in_dim(capacity, me * per_device, keepdims=False)
    row_index = jnp.arange(peer_count * buffer_rows, dtype=jnp.int32) % buffer_rows
    in_first = (row_index < first_cap)[:, None]
    act_here = jnp.where(in_first, first_act, second_act)
    act_all = lax.all_gather(act_here, "dp", axis=1, tiled=True)
    down_here = jnp.swapaxes(down_parts, 0, 1).reshape(per_device, -1, quarter)
    unit_count = down_weight.shape[1]
    first_sum = group_sums(act_all, down_here[0], unit_count)
    second_sum = group_sums(act_all, down_here[1], unit_count)
    expert_out = jnp.where(in_first, first_sum, second_sum).astype(jnp.bfloat16)
    summed = expert_out.reshape(peer_count, buffer_rows, quarter)
    (returned,) = exchange(summed, collective_id=1)

    flat_ret = returned.reshape(peer_count * buffer_rows, quarter)
    flat_ret = jnp.concatenate([flat_ret, jnp.zeros((1, quarter), flat_ret.dtype)])
    weight_kept = jnp.where(kept_mask, score, jnp.float32(0.0))
    gathered = flat_ret[target].astype(jnp.float32).reshape(rows_here, pick_count, quarter)
    mixture = jnp.sum(weight_kept.reshape(rows_here, pick_count)[:, :, None] * gathered, axis=1)
    residual = lax.dynamic_slice_in_dim(tokens, group_pos * quarter, quarter, 1).astype(jnp.float32)
    return (residual + mixture).astype(jnp.bfloat16)


def solution(mesh):
    in_specs = (
        P("expert", None),
        P(),
        P(),
        P("expert", None),
        P("expert", None),
        P(),
        P(),
        P("expert", None, None, "dp"),
        P("expert", "dp", None),
    )
    out_specs = P("expert", "dp")
    return jax.shard_map(
        on_device, mesh=mesh, in_specs=in_specs, out_specs=out_specs, check_vma=False
    )
```

```python
import functools

import jax
import jax.numpy as jnp
from jax import lax
from jax.experimental import pallas as pl
from jax.experimental.pallas import tpu as pltpu
from jax.sharding import PartitionSpec as P

MESH = pl.DeviceIdType.MESH

CAPACITY_HIGH = 16
CAP_DEV = 24
SEND_WINDOW = 8


def exchange_kernel(n_exp, n_dp, with_down, *refs):
    if with_down:
        send_ref, down_ref, recv_ref, down_out, a_send, a_recv, d_send, d_recv, local_sem = refs
    else:
        send_ref, recv_ref, a_send, a_recv, local_sem = refs
    me = lax.axis_index("expert")
    gi = lax.axis_index("dp")

    def a2a_copy(j, recv_slot):
        return pltpu.make_async_remote_copy(
            src_ref=send_ref.at[j],
            dst_ref=recv_ref.at[recv_slot],
            send_sem=a_send.at[j],
            recv_sem=a_recv.at[recv_slot],
            device_id=(gi, j),
            device_id_type=MESH,
        )

    def down_copy(g, recv_slot):
        q = down_out.shape[-1]
        cols = pl.ds(pl.multiple_of(g * q, 128), q)
        return pltpu.make_async_remote_copy(
            src_ref=down_ref.at[:, :, cols],
            dst_ref=down_out.at[recv_slot],
            send_sem=d_send.at[g],
            recv_sem=d_recv.at[recv_slot],
            device_id=(g, me),
            device_id_type=MESH,
        )

    barrier = pltpu.get_barrier_semaphore()

    def greet(k, carry):
        j = lax.rem(me + k, n_exp)
        pl.semaphore_signal(barrier, 1, device_id=(gi, j), device_id_type=MESH)
        return carry

    lax.fori_loop(1, n_exp, greet, 0)
    greet_count = n_exp - 1
    if with_down:
        for k in range(1, n_dp):
            g = lax.rem(gi + k, n_dp)
            pl.semaphore_signal(barrier, 1, device_id=(g, me), device_id_type=MESH)
        greet_count += n_dp - 1
    pl.semaphore_wait(barrier, greet_count)

    def send_one(k, carry):
        j = lax.rem(me + k, n_exp)
        a2a_copy(j, me).start()
        return carry

    lax.fori_loop(1, n_exp, send_one, 0)
    local = pltpu.make_async_copy(send_ref.at[me], recv_ref.at[me], local_sem.at[0])
    local.start()
    if with_down:
        q = down_out.shape[-1]
        for k in range(1, n_dp):
            down_copy(lax.rem(gi + k, n_dp), gi).start()
        own_cols = pl.ds(pl.multiple_of(gi * q, 128), q)
        local_down = pltpu.make_async_copy(
            down_ref.at[:, :, own_cols], down_out.at[gi], local_sem.at[1]
        )
        local_down.start()

    def wait_one(k, carry):
        j = lax.rem(me + k, n_exp)
        a2a_copy(j, me).wait_send()
        a2a_copy(j, j).wait_recv()
        return carry

    lax.fori_loop(1, n_exp, wait_one, 0)
    local.wait()
    if with_down:
        for k in range(1, n_dp):
            g = lax.rem(gi + k, n_dp)
            down_copy(g, gi).wait_send()
            down_copy(g, g).wait_recv()
        local_down.wait()


def exchange(send, down=None, collective_id=0):
    n_exp = lax.axis_size("expert")
    n_dp = lax.axis_size("dp")
    with_down = down is not None
    any_spec = pl.BlockSpec(memory_space=pl.ANY)
    out_shape = [jax.ShapeDtypeStruct(send.shape, send.dtype)]
    scratch = [pltpu.SemaphoreType.DMA((n_exp,)), pltpu.SemaphoreType.DMA((n_exp,))]
    operands = [send]
    moved = send.size * send.dtype.itemsize
    if with_down:
        q = down.shape[-1] // n_dp
        out_shape.append(jax.ShapeDtypeStruct((n_dp,) + down.shape[:-1] + (q,), down.dtype))
        scratch += [pltpu.SemaphoreType.DMA((n_dp,)), pltpu.SemaphoreType.DMA((n_dp,))]
        operands.append(down)
        moved += down.size * down.dtype.itemsize
    scratch.append(pltpu.SemaphoreType.DMA((2,)))
    return pl.pallas_call(
        functools.partial(exchange_kernel, n_exp, n_dp, with_down),
        out_shape=tuple(out_shape),
        in_specs=[any_spec] * len(operands),
        out_specs=tuple([any_spec] * len(out_shape)),
        scratch_shapes=scratch,
        compiler_params=pltpu.CompilerParams(collective_id=collective_id, has_side_effects=True),
        cost_estimate=pl.CostEstimate(flops=0, transcendentals=0, bytes_accessed=2 * moved),
    )(*operands)


def dispatch_kernel(n_exp, n_dp, send_ref, down_ref, full_ref, down_out,
                    a_send, a_recv, d_send, d_recv, f_send, f_recv, local_sem):
    me = lax.axis_index("expert")
    gi = lax.axis_index("dp")
    q = down_out.shape[-1]

    def a2a_copy(j, recv_slot):
        return pltpu.make_async_remote_copy(
            src_ref=send_ref.at[j],
            dst_ref=full_ref.at[gi, recv_slot],
            send_sem=a_send.at[j],
            recv_sem=a_recv.at[recv_slot],
            device_id=(gi, j),
            device_id_type=MESH,
        )

    def down_copy(g, recv_slot):
        cols = pl.ds(pl.multiple_of(g * q, 128), q)
        return pltpu.make_async_remote_copy(
            src_ref=down_ref.at[:, :, cols],
            dst_ref=down_out.at[recv_slot],
            send_sem=d_send.at[g],
            recv_sem=d_recv.at[recv_slot],
            device_id=(g, me),
            device_id_type=MESH,
        )

    def forward_copy(g, piece):
        return pltpu.make_async_remote_copy(
            src_ref=full_ref.at[gi, piece],
            dst_ref=full_ref.at[gi, piece],
            send_sem=f_send.at[g],
            recv_sem=f_recv.at[gi],
            device_id=(g, me),
            device_id_type=MESH,
        )

    def whole_from(g):
        return pltpu.make_async_remote_copy(
            src_ref=full_ref.at[gi],
            dst_ref=full_ref.at[g],
            send_sem=f_send.at[g],
            recv_sem=f_recv.at[g],
            device_id=(g, me),
            device_id_type=MESH,
        )

    barrier = pltpu.get_barrier_semaphore()

    def greet(k, carry):
        j = lax.rem(me + k, n_exp)
        pl.semaphore_signal(barrier, 1, device_id=(gi, j), device_id_type=MESH)
        return carry

    lax.fori_loop(1, n_exp, greet, 0)
    for k in range(1, n_dp):
        g = lax.rem(gi + k, n_dp)
        pl.semaphore_signal(barrier, 1, device_id=(g, me), device_id_type=MESH)
    pl.semaphore_wait(barrier, n_exp - 1 + n_dp - 1)

    window = min(SEND_WINDOW, n_exp - 1)
    for k in range(1, window + 1):
        a2a_copy(lax.rem(me + k, n_exp), me).start()
    local = pltpu.make_async_copy(send_ref.at[me], full_ref.at[gi, me], local_sem.at[0])
    local.start()
    for k in range(1, n_dp):
        down_copy(lax.rem(gi + k, n_dp), gi).start()
    own_cols = pl.ds(pl.multiple_of(gi * q, 128), q)
    local_down = pltpu.make_async_copy(down_ref.at[:, :, own_cols], down_out.at[gi], local_sem.at[1])
    local_down.start()

    local.wait()
    for k in range(1, n_dp):
        forward_copy(lax.rem(gi + k, n_dp), me).start()

    def take_one(k, carry):
        j = lax.rem(me - k + n_exp, n_exp)
        a2a_copy(j, j).wait_recv()
        for step in range(1, n_dp):
            forward_copy(lax.rem(gi + step, n_dp), j).start()

        @pl.when(k + window < n_exp)
        def _():
            a2a_copy(lax.rem(me + k + window, n_exp), me).start()

        return carry

    lax.fori_loop(1, n_exp, take_one, 0)

    def sent_one(k, carry):
        a2a_copy(lax.rem(me + k, n_exp), me).wait_send()
        return carry

    lax.fori_loop(1, n_exp, sent_one, 0)
    for k in range(1, n_dp):
        g = lax.rem(gi + k, n_dp)
        down_copy(g, gi).wait_send()
        down_copy(g, g).wait_recv()
        whole_from(g).wait_send()
        whole_from(g).wait_recv()
    local_down.wait()


def dispatch(send, down):
    n_exp = lax.axis_size("expert")
    n_dp = lax.axis_size("dp")
    q = down.shape[-1] // n_dp
    any_spec = pl.BlockSpec(memory_space=pl.ANY)
    moved = send.size * send.dtype.itemsize * n_dp + down.size * down.dtype.itemsize
    return pl.pallas_call(
        functools.partial(dispatch_kernel, n_exp, n_dp),
        out_shape=(
            jax.ShapeDtypeStruct((n_dp,) + send.shape, send.dtype),
            jax.ShapeDtypeStruct((n_dp,) + down.shape[:-1] + (q,), down.dtype),
        ),
        in_specs=[any_spec, any_spec],
        out_specs=(any_spec, any_spec),
        scratch_shapes=[
            pltpu.SemaphoreType.DMA((n_exp,)),
            pltpu.SemaphoreType.DMA((n_exp,)),
            pltpu.SemaphoreType.DMA((n_dp,)),
            pltpu.SemaphoreType.DMA((n_dp,)),
            pltpu.SemaphoreType.DMA((n_dp,)),
            pltpu.SemaphoreType.DMA((n_dp,)),
            pltpu.SemaphoreType.DMA((2,)),
        ],
        compiler_params=pltpu.CompilerParams(collective_id=2, has_side_effects=True),
        cost_estimate=pl.CostEstimate(flops=0, transcendentals=0, bytes_accessed=2 * moved),
    )(send, down)


def gather_kernel(n_dp, src_ref, out_ref, send_sem, recv_sem, local_sem):
    me = lax.axis_index("expert")
    gi = lax.axis_index("dp")

    def copy_to(g, recv_slot):
        return pltpu.make_async_remote_copy(
            src_ref=src_ref,
            dst_ref=out_ref.at[recv_slot],
            send_sem=send_sem.at[g],
            recv_sem=recv_sem.at[recv_slot],
            device_id=(g, me),
            device_id_type=MESH,
        )

    barrier = pltpu.get_barrier_semaphore()
    for k in range(1, n_dp):
        pl.semaphore_signal(barrier, 1, device_id=(lax.rem(gi + k, n_dp), me), device_id_type=MESH)
    pl.semaphore_wait(barrier, n_dp - 1)
    for k in range(1, n_dp):
        copy_to(lax.rem(gi + k, n_dp), gi).start()
    local = pltpu.make_async_copy(src_ref, out_ref.at[gi], local_sem.at[0])
    local.start()
    for k in range(1, n_dp):
        g = lax.rem(gi + k, n_dp)
        copy_to(g, gi).wait_send()
        copy_to(g, g).wait_recv()
    local.wait()


def gather_dp(src):
    n_dp = lax.axis_size("dp")
    any_spec = pl.BlockSpec(memory_space=pl.ANY)
    moved = src.size * src.dtype.itemsize * n_dp
    return pl.pallas_call(
        functools.partial(gather_kernel, n_dp),
        out_shape=jax.ShapeDtypeStruct((n_dp,) + src.shape, src.dtype),
        in_specs=[any_spec],
        out_specs=any_spec,
        scratch_shapes=[
            pltpu.SemaphoreType.DMA((n_dp,)),
            pltpu.SemaphoreType.DMA((n_dp,)),
            pltpu.SemaphoreType.DMA((1,)),
        ],
        compiler_params=pltpu.CompilerParams(collective_id=3, has_side_effects=True),
        cost_estimate=pl.CostEstimate(flops=0, transcendentals=0, bytes_accessed=2 * moved),
    )(src)


def assign_slots(experts, replica_key, slot_expert):
    flat_experts = experts.reshape(-1)
    holders = (flat_experts[:, None] == slot_expert[None, :]).astype(jnp.int32)
    copies = jnp.sum(holders, axis=1)
    earlier = jnp.cumsum(holders, axis=1) - holders
    wanted = replica_key.reshape(-1) % copies
    matched = holders * (earlier == wanted[:, None]).astype(jnp.int32)
    numbers = jnp.arange(slot_expert.shape[0], dtype=jnp.int32)
    return jnp.sum(matched * numbers[None, :], axis=1)


def slot_activated(quarters, gate_up_one):
    group_count, _, quarter = quarters.shape
    unit_count = gate_up_one.shape[2]
    gate_up_out = lax.dot_general(
        quarters,
        gate_up_one.reshape(group_count, quarter, 2 * unit_count),
        (((0, 2), (0, 1)), ((), ())),
        preferred_element_type=jnp.float32,
    )
    return (jax.nn.silu(gate_up_out[:, :unit_count]) * gate_up_out[:, unit_count:]).astype(
        jnp.bfloat16
    )


def group_sums(act_all, down_cols, unit_count):
    total = None
    for group in range(act_all.shape[0]):
        lower = group * unit_count
        piece = jnp.dot(
            act_all[group],
            down_cols[lower:lower + unit_count],
            preferred_element_type=jnp.float32,
        )
        piece = piece.astype(jnp.bfloat16).astype(jnp.float32)
        total = piece if total is None else total + piece
    return total


def on_device(
    tokens,
    norm_gain,
    routing_projection_matrix,
    experts,
    replica_key,
    slot_expert,
    capacity,
    slot_gate_up_weight,
    down_weight,
):
    peer_count = lax.axis_size("expert")
    group_count = lax.axis_size("dp")
    group_pos = lax.axis_index("dp")
    me = lax.axis_index("expert")
    rows_here = tokens.shape[0]
    model_width = tokens.shape[1]
    pick_count = experts.shape[1]
    slot_count = slot_expert.shape[0]
    per_device = slot_count // peer_count
    quarter = model_width // group_count
    buffer_rows = CAP_DEV

    hidden = tokens.astype(jnp.float32)
    scale = lax.rsqrt(jnp.mean(hidden * hidden, axis=-1, keepdims=True) + 1e-06)
    normed = (hidden * scale * norm_gain.astype(jnp.float32)).astype(jnp.bfloat16)
    logits = jnp.dot(normed, routing_projection_matrix, preferred_element_type=jnp.float32)
    score = jax.nn.sigmoid(jnp.take_along_axis(logits, experts, axis=1)).reshape(-1)

    slot_ids = assign_slots(experts, replica_key, slot_expert)
    onehot = (slot_ids[:, None] == jnp.arange(slot_count, dtype=jnp.int32)[None, :]).astype(
        jnp.int32
    )
    position = jnp.sum((jnp.cumsum(onehot, axis=0) - onehot) * onehot, axis=1)
    slot_cap = jnp.sum(onehot * capacity[None, :], axis=1)
    kept_mask = position < slot_cap
    is_second = (slot_ids % per_device) == 1
    row_in = jnp.where(is_second, buffer_rows - slot_cap + position, position)
    target = jnp.where(
        kept_mask, slot_ids // per_device * buffer_rows + row_in, peer_count * buffer_rows
    )
    source_rows = jnp.arange(rows_here * pick_count, dtype=jnp.int32) // pick_count

    normed_part = lax.dynamic_slice_in_dim(normed, group_pos * quarter, quarter, 1)
    outgoing = (
        jnp.zeros((peer_count * buffer_rows + 1, quarter), jnp.bfloat16)
        .at[target]
        .set(normed_part[source_rows])
    )
    outgoing = outgoing[:-1].reshape(peer_count, buffer_rows, quarter)
    full_in, down_parts = dispatch(outgoing, down_weight)
    quarters = full_in.reshape(group_count, peer_count * buffer_rows, quarter)

    first_act = slot_activated(quarters, slot_gate_up_weight[0])
    second_act = slot_activated(quarters, slot_gate_up_weight[1])
    first_cap = lax.dynamic_index_in_dim(capacity, me * per_device, keepdims=False)
    row_index = jnp.arange(peer_count * buffer_rows, dtype=jnp.int32) % buffer_rows
    in_first = (row_index < first_cap)[:, None]
    act_here = jnp.where(in_first, first_act, second_act)
    act_all = gather_dp(act_here)
    down_here = jnp.swapaxes(down_parts, 0, 1).reshape(per_device, -1, quarter)
    unit_count = down_weight.shape[1]
    first_sum = group_sums(act_all, down_here[0], unit_count)
    second_sum = group_sums(act_all, down_here[1], unit_count)
    expert_out = jnp.where(in_first, first_sum, second_sum).astype(jnp.bfloat16)
    summed = expert_out.reshape(peer_count, buffer_rows, quarter)
    (returned,) = exchange(summed, collective_id=1)

    flat_ret = returned.reshape(peer_count * buffer_rows, quarter)
    flat_ret = jnp.concatenate([flat_ret, jnp.zeros((1, quarter), flat_ret.dtype)])
    weight_kept = jnp.where(kept_mask, score, jnp.float32(0.0))
    gathered = flat_ret[target].astype(jnp.float32).reshape(rows_here, pick_count, quarter)
    mixture = jnp.sum(weight_kept.reshape(rows_here, pick_count)[:, :, None] * gathered, axis=1)
    residual = lax.dynamic_slice_in_dim(tokens, group_pos * quarter, quarter, 1).astype(jnp.float32)
    return (residual + mixture).astype(jnp.bfloat16)


def solution(mesh):
    in_specs = (
        P("expert", None),
        P(),
        P(),
        P("expert", None),
        P("expert", None),
        P(),
        P(),
        P("expert", None, None, "dp"),
        P("expert", "dp", None),
    )
    out_specs = P("expert", "dp")
    return jax.shard_map(
        on_device, mesh=mesh, in_specs=in_specs, out_specs=out_specs, check_vma=False
    )
```

```python
import functools

import jax
import jax.numpy as jnp
from jax import lax
from jax.experimental import pallas as pl
from jax.experimental.pallas import tpu as pltpu
from jax.sharding import PartitionSpec as P

MESH = pl.DeviceIdType.MESH

CAPACITY_HIGH = 16
CAP_DEV = 24
SEND_WINDOW = 8


def exchange_kernel(n_exp, n_dp, with_down, *refs):
    if with_down:
        send_ref, down_ref, recv_ref, down_out, a_send, a_recv, d_send, d_recv, local_sem = refs
    else:
        send_ref, recv_ref, a_send, a_recv, local_sem = refs
    me = lax.axis_index("expert")
    gi = lax.axis_index("dp")

    def a2a_copy(j, recv_slot):
        return pltpu.make_async_remote_copy(
            src_ref=send_ref.at[j],
            dst_ref=recv_ref.at[recv_slot],
            send_sem=a_send.at[j],
            recv_sem=a_recv.at[recv_slot],
            device_id=(gi, j),
            device_id_type=MESH,
        )

    def down_copy(g, recv_slot):
        q = down_out.shape[-1]
        cols = pl.ds(pl.multiple_of(g * q, 128), q)
        return pltpu.make_async_remote_copy(
            src_ref=down_ref.at[:, :, cols],
            dst_ref=down_out.at[recv_slot],
            send_sem=d_send.at[g],
            recv_sem=d_recv.at[recv_slot],
            device_id=(g, me),
            device_id_type=MESH,
        )

    barrier = pltpu.get_barrier_semaphore()

    def greet(k, carry):
        j = lax.rem(me + k, n_exp)
        pl.semaphore_signal(barrier, 1, device_id=(gi, j), device_id_type=MESH)
        return carry

    lax.fori_loop(1, n_exp, greet, 0)
    greet_count = n_exp - 1
    if with_down:
        for k in range(1, n_dp):
            g = lax.rem(gi + k, n_dp)
            pl.semaphore_signal(barrier, 1, device_id=(g, me), device_id_type=MESH)
        greet_count += n_dp - 1
    pl.semaphore_wait(barrier, greet_count)

    def send_one(k, carry):
        j = lax.rem(me + k, n_exp)
        a2a_copy(j, me).start()
        return carry

    lax.fori_loop(1, n_exp, send_one, 0)
    local = pltpu.make_async_copy(send_ref.at[me], recv_ref.at[me], local_sem.at[0])
    local.start()
    if with_down:
        q = down_out.shape[-1]
        for k in range(1, n_dp):
            down_copy(lax.rem(gi + k, n_dp), gi).start()
        own_cols = pl.ds(pl.multiple_of(gi * q, 128), q)
        local_down = pltpu.make_async_copy(
            down_ref.at[:, :, own_cols], down_out.at[gi], local_sem.at[1]
        )
        local_down.start()

    def wait_one(k, carry):
        j = lax.rem(me + k, n_exp)
        a2a_copy(j, me).wait_send()
        a2a_copy(j, j).wait_recv()
        return carry

    lax.fori_loop(1, n_exp, wait_one, 0)
    local.wait()
    if with_down:
        for k in range(1, n_dp):
            g = lax.rem(gi + k, n_dp)
            down_copy(g, gi).wait_send()
            down_copy(g, g).wait_recv()
        local_down.wait()


def exchange(send, down=None, collective_id=0):
    n_exp = lax.axis_size("expert")
    n_dp = lax.axis_size("dp")
    with_down = down is not None
    any_spec = pl.BlockSpec(memory_space=pl.ANY)
    out_shape = [jax.ShapeDtypeStruct(send.shape, send.dtype)]
    scratch = [pltpu.SemaphoreType.DMA((n_exp,)), pltpu.SemaphoreType.DMA((n_exp,))]
    operands = [send]
    moved = send.size * send.dtype.itemsize
    if with_down:
        q = down.shape[-1] // n_dp
        out_shape.append(jax.ShapeDtypeStruct((n_dp,) + down.shape[:-1] + (q,), down.dtype))
        scratch += [pltpu.SemaphoreType.DMA((n_dp,)), pltpu.SemaphoreType.DMA((n_dp,))]
        operands.append(down)
        moved += down.size * down.dtype.itemsize
    scratch.append(pltpu.SemaphoreType.DMA((2,)))
    return pl.pallas_call(
        functools.partial(exchange_kernel, n_exp, n_dp, with_down),
        out_shape=tuple(out_shape),
        in_specs=[any_spec] * len(operands),
        out_specs=tuple([any_spec] * len(out_shape)),
        scratch_shapes=scratch,
        compiler_params=pltpu.CompilerParams(collective_id=collective_id, has_side_effects=True),
        cost_estimate=pl.CostEstimate(flops=0, transcendentals=0, bytes_accessed=2 * moved),
    )(*operands)


def dispatch_kernel(n_exp, n_dp, send_ref, down_ref, full_ref, down_out,
                    a_send, a_recv, d_send, d_recv, n_send, lo_recv, hi_recv,
                    r_send, r_recv, local_sem):
    me = lax.axis_index("expert")
    gi = lax.axis_index("dp")
    q = down_out.shape[-1]
    half = full_ref.shape[-1] // 2
    lo = lax.rem(gi + n_dp - 1, n_dp)
    hi = lax.rem(gi + 1, n_dp)
    far = lax.rem(gi + 2, n_dp)
    first = pl.ds(0, half)
    second = pl.ds(half, half)

    def a2a_copy(j, recv_slot):
        return pltpu.make_async_remote_copy(
            src_ref=send_ref.at[j],
            dst_ref=full_ref.at[gi, recv_slot],
            send_sem=a_send.at[j],
            recv_sem=a_recv.at[recv_slot],
            device_id=(gi, j),
            device_id_type=MESH,
        )

    def down_copy(g, recv_slot):
        cols = pl.ds(pl.multiple_of(g * q, 128), q)
        return pltpu.make_async_remote_copy(
            src_ref=down_ref.at[:, :, cols],
            dst_ref=down_out.at[recv_slot],
            send_sem=d_send.at[g],
            recv_sem=d_recv.at[recv_slot],
            device_id=(g, me),
            device_id_type=MESH,
        )

    def to_hi(piece):
        return pltpu.make_async_remote_copy(
            src_ref=full_ref.at[gi, piece],
            dst_ref=full_ref.at[gi, piece],
            send_sem=n_send.at[1],
            recv_sem=lo_recv.at[piece],
            device_id=(hi, me),
            device_id_type=MESH,
        )

    def to_lo(piece):
        return pltpu.make_async_remote_copy(
            src_ref=full_ref.at[gi, piece],
            dst_ref=full_ref.at[gi, piece],
            send_sem=n_send.at[0],
            recv_sem=hi_recv.at[piece],
            device_id=(lo, me),
            device_id_type=MESH,
        )

    def from_lo(piece):
        return pltpu.make_async_remote_copy(
            src_ref=full_ref.at[lo, piece],
            dst_ref=full_ref.at[lo, piece],
            send_sem=n_send.at[0],
            recv_sem=lo_recv.at[piece],
            device_id=(lo, me),
            device_id_type=MESH,
        )

    def from_hi(piece):
        return pltpu.make_async_remote_copy(
            src_ref=full_ref.at[hi, piece],
            dst_ref=full_ref.at[hi, piece],
            send_sem=n_send.at[1],
            recv_sem=hi_recv.at[piece],
            device_id=(hi, me),
            device_id_type=MESH,
        )

    def relay_up(piece):
        return pltpu.make_async_remote_copy(
            src_ref=full_ref.at[lo, piece, :, first],
            dst_ref=full_ref.at[lo, piece, :, first],
            send_sem=r_send.at[1],
            recv_sem=r_recv.at[0],
            device_id=(hi, me),
            device_id_type=MESH,
        )

    def relay_down(piece):
        return pltpu.make_async_remote_copy(
            src_ref=full_ref.at[hi, piece, :, second],
            dst_ref=full_ref.at[hi, piece, :, second],
            send_sem=r_send.at[0],
            recv_sem=r_recv.at[1],
            device_id=(lo, me),
            device_id_type=MESH,
        )

    barrier = pltpu.get_barrier_semaphore()

    def greet(k, carry):
        j = lax.rem(me + k, n_exp)
        pl.semaphore_signal(barrier, 1, device_id=(gi, j), device_id_type=MESH)
        return carry

    lax.fori_loop(1, n_exp, greet, 0)
    for k in range(1, n_dp):
        g = lax.rem(gi + k, n_dp)
        pl.semaphore_signal(barrier, 1, device_id=(g, me), device_id_type=MESH)
    pl.semaphore_wait(barrier, n_exp - 1 + n_dp - 1)

    window = min(SEND_WINDOW, n_exp - 1)
    for k in range(1, window + 1):
        a2a_copy(lax.rem(me + k, n_exp), me).start()
    local = pltpu.make_async_copy(send_ref.at[me], full_ref.at[gi, me], local_sem.at[0])
    local.start()
    for k in range(1, n_dp):
        down_copy(lax.rem(gi + k, n_dp), gi).start()
    own_cols = pl.ds(pl.multiple_of(gi * q, 128), q)
    local_down = pltpu.make_async_copy(down_ref.at[:, :, own_cols], down_out.at[gi], local_sem.at[1])
    local_down.start()

    local.wait()
    to_hi(me).start()
    to_lo(me).start()

    def take_one(k, carry):
        j = lax.rem(me - k + n_exp, n_exp)
        a2a_copy(j, j).wait_recv()
        to_hi(j).start()
        to_lo(j).start()

        @pl.when(k + window < n_exp)
        def _():
            a2a_copy(lax.rem(me + k + window, n_exp), me).start()

        return carry

    lax.fori_loop(1, n_exp, take_one, 0)

    def relay_one(k, carry):
        j = lax.rem(me - k + n_exp, n_exp)
        from_lo(j).wait_recv()
        relay_up(j).start()
        from_hi(j).wait_recv()
        relay_down(j).start()
        return carry

    lax.fori_loop(0, n_exp, relay_one, 0)

    def sent_one(k, carry):
        a2a_copy(lax.rem(me + k, n_exp), me).wait_send()
        return carry

    lax.fori_loop(1, n_exp, sent_one, 0)
    for k in range(1, n_dp):
        g = lax.rem(gi + k, n_dp)
        down_copy(g, gi).wait_send()
        down_copy(g, g).wait_recv()
    local_down.wait()
    pltpu.make_async_remote_copy(
        src_ref=full_ref.at[gi], dst_ref=full_ref.at[gi], send_sem=n_send.at[1],
        recv_sem=lo_recv.at[0], device_id=(hi, me), device_id_type=MESH,
    ).wait_send()
    pltpu.make_async_remote_copy(
        src_ref=full_ref.at[gi], dst_ref=full_ref.at[gi], send_sem=n_send.at[0],
        recv_sem=hi_recv.at[0], device_id=(lo, me), device_id_type=MESH,
    ).wait_send()
    pltpu.make_async_remote_copy(
        src_ref=full_ref.at[lo, :, :, first], dst_ref=full_ref.at[lo, :, :, first],
        send_sem=r_send.at[1], recv_sem=r_recv.at[0], device_id=(hi, me), device_id_type=MESH,
    ).wait_send()
    pltpu.make_async_remote_copy(
        src_ref=full_ref.at[hi, :, :, second], dst_ref=full_ref.at[hi, :, :, second],
        send_sem=r_send.at[0], recv_sem=r_recv.at[1], device_id=(lo, me), device_id_type=MESH,
    ).wait_send()
    pltpu.make_async_remote_copy(
        src_ref=full_ref.at[far, :, :, first], dst_ref=full_ref.at[far, :, :, first],
        send_sem=r_send.at[1], recv_sem=r_recv.at[0], device_id=(hi, me), device_id_type=MESH,
    ).wait_recv()
    pltpu.make_async_remote_copy(
        src_ref=full_ref.at[far, :, :, second], dst_ref=full_ref.at[far, :, :, second],
        send_sem=r_send.at[0], recv_sem=r_recv.at[1], device_id=(lo, me), device_id_type=MESH,
    ).wait_recv()


def dispatch(send, down):
    n_exp = lax.axis_size("expert")
    n_dp = lax.axis_size("dp")
    q = down.shape[-1] // n_dp
    any_spec = pl.BlockSpec(memory_space=pl.ANY)
    moved = send.size * send.dtype.itemsize * n_dp + down.size * down.dtype.itemsize
    return pl.pallas_call(
        functools.partial(dispatch_kernel, n_exp, n_dp),
        out_shape=(
            jax.ShapeDtypeStruct((n_dp,) + send.shape, send.dtype),
            jax.ShapeDtypeStruct((n_dp,) + down.shape[:-1] + (q,), down.dtype),
        ),
        in_specs=[any_spec, any_spec],
        out_specs=(any_spec, any_spec),
        scratch_shapes=[
            pltpu.SemaphoreType.DMA((n_exp,)),
            pltpu.SemaphoreType.DMA((n_exp,)),
            pltpu.SemaphoreType.DMA((n_dp,)),
            pltpu.SemaphoreType.DMA((n_dp,)),
            pltpu.SemaphoreType.DMA((2,)),
            pltpu.SemaphoreType.DMA((n_exp,)),
            pltpu.SemaphoreType.DMA((n_exp,)),
            pltpu.SemaphoreType.DMA((2,)),
            pltpu.SemaphoreType.DMA((2,)),
            pltpu.SemaphoreType.DMA((2,)),
        ],
        compiler_params=pltpu.CompilerParams(collective_id=2, has_side_effects=True),
        cost_estimate=pl.CostEstimate(flops=0, transcendentals=0, bytes_accessed=2 * moved),
    )(send, down)


def gather_kernel(n_dp, src_ref, out_ref, send_sem, recv_sem, local_sem):
    me = lax.axis_index("expert")
    gi = lax.axis_index("dp")

    def copy_to(g, recv_slot):
        return pltpu.make_async_remote_copy(
            src_ref=src_ref,
            dst_ref=out_ref.at[recv_slot],
            send_sem=send_sem.at[g],
            recv_sem=recv_sem.at[recv_slot],
            device_id=(g, me),
            device_id_type=MESH,
        )

    barrier = pltpu.get_barrier_semaphore()
    for k in range(1, n_dp):
        pl.semaphore_signal(barrier, 1, device_id=(lax.rem(gi + k, n_dp), me), device_id_type=MESH)
    pl.semaphore_wait(barrier, n_dp - 1)
    for k in range(1, n_dp):
        copy_to(lax.rem(gi + k, n_dp), gi).start()
    local = pltpu.make_async_copy(src_ref, out_ref.at[gi], local_sem.at[0])
    local.start()
    for k in range(1, n_dp):
        g = lax.rem(gi + k, n_dp)
        copy_to(g, gi).wait_send()
        copy_to(g, g).wait_recv()
    local.wait()


def gather_dp(src):
    n_dp = lax.axis_size("dp")
    any_spec = pl.BlockSpec(memory_space=pl.ANY)
    moved = src.size * src.dtype.itemsize * n_dp
    return pl.pallas_call(
        functools.partial(gather_kernel, n_dp),
        out_shape=jax.ShapeDtypeStruct((n_dp,) + src.shape, src.dtype),
        in_specs=[any_spec],
        out_specs=any_spec,
        scratch_shapes=[
            pltpu.SemaphoreType.DMA((n_dp,)),
            pltpu.SemaphoreType.DMA((n_dp,)),
            pltpu.SemaphoreType.DMA((1,)),
        ],
        compiler_params=pltpu.CompilerParams(collective_id=3, has_side_effects=True),
        cost_estimate=pl.CostEstimate(flops=0, transcendentals=0, bytes_accessed=2 * moved),
    )(src)


def assign_slots(experts, replica_key, slot_expert):
    flat_experts = experts.reshape(-1)
    holders = (flat_experts[:, None] == slot_expert[None, :]).astype(jnp.int32)
    copies = jnp.sum(holders, axis=1)
    earlier = jnp.cumsum(holders, axis=1) - holders
    wanted = replica_key.reshape(-1) % copies
    matched = holders * (earlier == wanted[:, None]).astype(jnp.int32)
    numbers = jnp.arange(slot_expert.shape[0], dtype=jnp.int32)
    return jnp.sum(matched * numbers[None, :], axis=1)


def slot_activated(quarters, gate_up_one):
    group_count, _, quarter = quarters.shape
    unit_count = gate_up_one.shape[2]
    gate_up_out = lax.dot_general(
        quarters,
        gate_up_one.reshape(group_count, quarter, 2 * unit_count),
        (((0, 2), (0, 1)), ((), ())),
        preferred_element_type=jnp.float32,
    )
    return (jax.nn.silu(gate_up_out[:, :unit_count]) * gate_up_out[:, unit_count:]).astype(
        jnp.bfloat16
    )


def group_sums(act_all, down_cols, unit_count):
    total = None
    for group in range(act_all.shape[0]):
        lower = group * unit_count
        piece = jnp.dot(
            act_all[group],
            down_cols[lower:lower + unit_count],
            preferred_element_type=jnp.float32,
        )
        piece = piece.astype(jnp.bfloat16).astype(jnp.float32)
        total = piece if total is None else total + piece
    return total


def on_device(
    tokens,
    norm_gain,
    routing_projection_matrix,
    experts,
    replica_key,
    slot_expert,
    capacity,
    slot_gate_up_weight,
    down_weight,
):
    peer_count = lax.axis_size("expert")
    group_count = lax.axis_size("dp")
    group_pos = lax.axis_index("dp")
    me = lax.axis_index("expert")
    rows_here = tokens.shape[0]
    model_width = tokens.shape[1]
    pick_count = experts.shape[1]
    slot_count = slot_expert.shape[0]
    per_device = slot_count // peer_count
    quarter = model_width // group_count
    buffer_rows = CAP_DEV

    hidden = tokens.astype(jnp.float32)
    scale = lax.rsqrt(jnp.mean(hidden * hidden, axis=-1, keepdims=True) + 1e-06)
    normed = (hidden * scale * norm_gain.astype(jnp.float32)).astype(jnp.bfloat16)
    logits = jnp.dot(normed, routing_projection_matrix, preferred_element_type=jnp.float32)
    score = jax.nn.sigmoid(jnp.take_along_axis(logits, experts, axis=1)).reshape(-1)

    slot_ids = assign_slots(experts, replica_key, slot_expert)
    onehot = (slot_ids[:, None] == jnp.arange(slot_count, dtype=jnp.int32)[None, :]).astype(
        jnp.int32
    )
    position = jnp.sum((jnp.cumsum(onehot, axis=0) - onehot) * onehot, axis=1)
    slot_cap = jnp.sum(onehot * capacity[None, :], axis=1)
    kept_mask = position < slot_cap
    is_second = (slot_ids % per_device) == 1
    row_in = jnp.where(is_second, buffer_rows - slot_cap + position, position)
    target = jnp.where(
        kept_mask, slot_ids // per_device * buffer_rows + row_in, peer_count * buffer_rows
    )
    source_rows = jnp.arange(rows_here * pick_count, dtype=jnp.int32) // pick_count

    normed_part = lax.dynamic_slice_in_dim(normed, group_pos * quarter, quarter, 1)
    outgoing = (
        jnp.zeros((peer_count * buffer_rows + 1, quarter), jnp.bfloat16)
        .at[target]
        .set(normed_part[source_rows])
    )
    outgoing = outgoing[:-1].reshape(peer_count, buffer_rows, quarter)
    full_in, down_parts = dispatch(outgoing, down_weight)
    quarters = full_in.reshape(group_count, peer_count * buffer_rows, quarter)

    first_act = slot_activated(quarters, slot_gate_up_weight[0])
    second_act = slot_activated(quarters, slot_gate_up_weight[1])
    first_cap = lax.dynamic_index_in_dim(capacity, me * per_device, keepdims=False)
    row_index = jnp.arange(peer_count * buffer_rows, dtype=jnp.int32) % buffer_rows
    in_first = (row_index < first_cap)[:, None]
    act_here = jnp.where(in_first, first_act, second_act)
    act_all = gather_dp(act_here)
    down_here = jnp.swapaxes(down_parts, 0, 1).reshape(per_device, -1, quarter)
    unit_count = down_weight.shape[1]
    first_sum = group_sums(act_all, down_here[0], unit_count)
    second_sum = group_sums(act_all, down_here[1], unit_count)
    expert_out = jnp.where(in_first, first_sum, second_sum).astype(jnp.bfloat16)
    summed = expert_out.reshape(peer_count, buffer_rows, quarter)
    (returned,) = exchange(summed, collective_id=1)

    flat_ret = returned.reshape(peer_count * buffer_rows, quarter)
    flat_ret = jnp.concatenate([flat_ret, jnp.zeros((1, quarter), flat_ret.dtype)])
    weight_kept = jnp.where(kept_mask, score, jnp.float32(0.0))
    gathered = flat_ret[target].astype(jnp.float32).reshape(rows_here, pick_count, quarter)
    mixture = jnp.sum(weight_kept.reshape(rows_here, pick_count)[:, :, None] * gathered, axis=1)
    residual = lax.dynamic_slice_in_dim(tokens, group_pos * quarter, quarter, 1).astype(jnp.float32)
    return (residual + mixture).astype(jnp.bfloat16)


def solution(mesh):
    in_specs = (
        P("expert", None),
        P(),
        P(),
        P("expert", None),
        P("expert", None),
        P(),
        P(),
        P("expert", None, None, "dp"),
        P("expert", "dp", None),
    )
    out_specs = P("expert", "dp")
    return jax.shard_map(
        on_device, mesh=mesh, in_specs=in_specs, out_specs=out_specs, check_vma=False
    )
```

```python
import functools

import jax
import jax.numpy as jnp
from jax import lax
from jax.experimental import pallas as pl
from jax.experimental.pallas import tpu as pltpu
from jax.sharding import PartitionSpec as P

MESH = pl.DeviceIdType.MESH

CAPACITY_HIGH = 16
CAP_DEV = 24
SEND_WINDOW = 8


def exchange_kernel(n_exp, n_dp, with_down, *refs):
    if with_down:
        send_ref, down_ref, recv_ref, down_out, a_send, a_recv, d_send, d_recv, local_sem = refs
    else:
        send_ref, recv_ref, a_send, a_recv, local_sem = refs
    me = lax.axis_index("expert")
    gi = lax.axis_index("dp")

    def a2a_copy(j, recv_slot):
        return pltpu.make_async_remote_copy(
            src_ref=send_ref.at[j],
            dst_ref=recv_ref.at[recv_slot],
            send_sem=a_send.at[j],
            recv_sem=a_recv.at[recv_slot],
            device_id=(gi, j),
            device_id_type=MESH,
        )

    def down_copy(g, recv_slot):
        q = down_out.shape[-1]
        cols = pl.ds(pl.multiple_of(g * q, 128), q)
        return pltpu.make_async_remote_copy(
            src_ref=down_ref.at[:, :, cols],
            dst_ref=down_out.at[recv_slot],
            send_sem=d_send.at[g],
            recv_sem=d_recv.at[recv_slot],
            device_id=(g, me),
            device_id_type=MESH,
        )

    barrier = pltpu.get_barrier_semaphore()

    def greet(k, carry):
        j = lax.rem(me + k, n_exp)
        pl.semaphore_signal(barrier, 1, device_id=(gi, j), device_id_type=MESH)
        return carry

    lax.fori_loop(1, n_exp, greet, 0)
    greet_count = n_exp - 1
    if with_down:
        for k in range(1, n_dp):
            g = lax.rem(gi + k, n_dp)
            pl.semaphore_signal(barrier, 1, device_id=(g, me), device_id_type=MESH)
        greet_count += n_dp - 1
    pl.semaphore_wait(barrier, greet_count)

    def send_one(k, carry):
        j = lax.rem(me + k, n_exp)
        a2a_copy(j, me).start()
        return carry

    lax.fori_loop(1, n_exp, send_one, 0)
    local = pltpu.make_async_copy(send_ref.at[me], recv_ref.at[me], local_sem.at[0])
    local.start()
    if with_down:
        q = down_out.shape[-1]
        for k in range(1, n_dp):
            down_copy(lax.rem(gi + k, n_dp), gi).start()
        own_cols = pl.ds(pl.multiple_of(gi * q, 128), q)
        local_down = pltpu.make_async_copy(
            down_ref.at[:, :, own_cols], down_out.at[gi], local_sem.at[1]
        )
        local_down.start()

    def wait_one(k, carry):
        j = lax.rem(me + k, n_exp)
        a2a_copy(j, me).wait_send()
        a2a_copy(j, j).wait_recv()
        return carry

    lax.fori_loop(1, n_exp, wait_one, 0)
    local.wait()
    if with_down:
        for k in range(1, n_dp):
            g = lax.rem(gi + k, n_dp)
            down_copy(g, gi).wait_send()
            down_copy(g, g).wait_recv()
        local_down.wait()


def exchange(send, down=None, collective_id=0):
    n_exp = lax.axis_size("expert")
    n_dp = lax.axis_size("dp")
    with_down = down is not None
    any_spec = pl.BlockSpec(memory_space=pl.ANY)
    out_shape = [jax.ShapeDtypeStruct(send.shape, send.dtype)]
    scratch = [pltpu.SemaphoreType.DMA((n_exp,)), pltpu.SemaphoreType.DMA((n_exp,))]
    operands = [send]
    moved = send.size * send.dtype.itemsize
    if with_down:
        q = down.shape[-1] // n_dp
        out_shape.append(jax.ShapeDtypeStruct((n_dp,) + down.shape[:-1] + (q,), down.dtype))
        scratch += [pltpu.SemaphoreType.DMA((n_dp,)), pltpu.SemaphoreType.DMA((n_dp,))]
        operands.append(down)
        moved += down.size * down.dtype.itemsize
    scratch.append(pltpu.SemaphoreType.DMA((2,)))
    return pl.pallas_call(
        functools.partial(exchange_kernel, n_exp, n_dp, with_down),
        out_shape=tuple(out_shape),
        in_specs=[any_spec] * len(operands),
        out_specs=tuple([any_spec] * len(out_shape)),
        scratch_shapes=scratch,
        compiler_params=pltpu.CompilerParams(collective_id=collective_id, has_side_effects=True),
        cost_estimate=pl.CostEstimate(flops=0, transcendentals=0, bytes_accessed=2 * moved),
    )(*operands)


def dispatch_kernel(n_exp, n_dp, send_ref, down_ref, full_ref, down_out,
                    a_send, a_recv, d_send, d_recv, n_send, lo_recv, hi_recv,
                    r_send, r_recv, local_sem):
    me = lax.axis_index("expert")
    gi = lax.axis_index("dp")
    q = down_out.shape[-1]
    half = full_ref.shape[-1] // 2
    lo = lax.rem(gi + n_dp - 1, n_dp)
    hi = lax.rem(gi + 1, n_dp)
    far = lax.rem(gi + 2, n_dp)
    first = pl.ds(0, half)
    second = pl.ds(half, half)

    def a2a_copy(j, recv_slot):
        return pltpu.make_async_remote_copy(
            src_ref=send_ref.at[j],
            dst_ref=full_ref.at[gi, recv_slot],
            send_sem=a_send.at[j],
            recv_sem=a_recv.at[recv_slot],
            device_id=(gi, j),
            device_id_type=MESH,
        )

    def down_copy(g, recv_slot):
        cols = pl.ds(pl.multiple_of(g * q, 128), q)
        return pltpu.make_async_remote_copy(
            src_ref=down_ref.at[:, :, cols],
            dst_ref=down_out.at[recv_slot],
            send_sem=d_send.at[g],
            recv_sem=d_recv.at[recv_slot],
            device_id=(g, me),
            device_id_type=MESH,
        )

    def to_hi(piece):
        return pltpu.make_async_remote_copy(
            src_ref=full_ref.at[gi, piece],
            dst_ref=full_ref.at[gi, piece],
            send_sem=n_send.at[1],
            recv_sem=lo_recv.at[piece],
            device_id=(hi, me),
            device_id_type=MESH,
        )

    def to_lo(piece):
        return pltpu.make_async_remote_copy(
            src_ref=full_ref.at[gi, piece],
            dst_ref=full_ref.at[gi, piece],
            send_sem=n_send.at[0],
            recv_sem=hi_recv.at[piece],
            device_id=(lo, me),
            device_id_type=MESH,
        )

    def from_lo(piece):
        return pltpu.make_async_remote_copy(
            src_ref=full_ref.at[lo, piece],
            dst_ref=full_ref.at[lo, piece],
            send_sem=n_send.at[0],
            recv_sem=lo_recv.at[piece],
            device_id=(lo, me),
            device_id_type=MESH,
        )

    def from_hi(piece):
        return pltpu.make_async_remote_copy(
            src_ref=full_ref.at[hi, piece],
            dst_ref=full_ref.at[hi, piece],
            send_sem=n_send.at[1],
            recv_sem=hi_recv.at[piece],
            device_id=(hi, me),
            device_id_type=MESH,
        )

    def relay_up(piece):
        return pltpu.make_async_remote_copy(
            src_ref=full_ref.at[lo, piece, :, first],
            dst_ref=full_ref.at[lo, piece, :, first],
            send_sem=r_send.at[1],
            recv_sem=r_recv.at[0],
            device_id=(hi, me),
            device_id_type=MESH,
        )

    def relay_down(piece):
        return pltpu.make_async_remote_copy(
            src_ref=full_ref.at[hi, piece, :, second],
            dst_ref=full_ref.at[hi, piece, :, second],
            send_sem=r_send.at[0],
            recv_sem=r_recv.at[1],
            device_id=(lo, me),
            device_id_type=MESH,
        )

    barrier = pltpu.get_barrier_semaphore()

    def greet(k, carry):
        j = lax.rem(me + k, n_exp)
        pl.semaphore_signal(barrier, 1, device_id=(gi, j), device_id_type=MESH)
        return carry

    lax.fori_loop(1, n_exp, greet, 0)
    for k in range(1, n_dp):
        g = lax.rem(gi + k, n_dp)
        pl.semaphore_signal(barrier, 1, device_id=(g, me), device_id_type=MESH)
    pl.semaphore_wait(barrier, n_exp - 1 + n_dp - 1)

    window = min(SEND_WINDOW, n_exp - 1)
    for k in range(1, window + 1):
        a2a_copy(lax.rem(me + k, n_exp), me).start()
    local = pltpu.make_async_copy(send_ref.at[me], full_ref.at[gi, me], local_sem.at[0])
    local.start()
    for k in range(1, n_dp):
        down_copy(lax.rem(gi + k, n_dp), gi).start()
    own_cols = pl.ds(pl.multiple_of(gi * q, 128), q)
    local_down = pltpu.make_async_copy(down_ref.at[:, :, own_cols], down_out.at[gi], local_sem.at[1])
    local_down.start()

    local.wait()
    to_hi(me).start()
    to_lo(me).start()

    def take_one(k, carry):
        j = lax.rem(me - k + n_exp, n_exp)
        a2a_copy(j, j).wait_recv()
        to_hi(j).start()
        to_lo(j).start()

        @pl.when(k + window < n_exp)
        def _():
            a2a_copy(lax.rem(me + k + window, n_exp), me).start()

        return carry

    lax.fori_loop(1, n_exp, take_one, 0)

    def relay_one(k, carry):
        j = lax.rem(me - k + n_exp, n_exp)
        from_lo(j).wait_recv()
        relay_up(j).start()
        from_hi(j).wait_recv()
        relay_down(j).start()
        return carry

    lax.fori_loop(0, n_exp, relay_one, 0)

    def sent_one(k, carry):
        a2a_copy(lax.rem(me + k, n_exp), me).wait_send()
        return carry

    lax.fori_loop(1, n_exp, sent_one, 0)
    for k in range(1, n_dp):
        g = lax.rem(gi + k, n_dp)
        down_copy(g, gi).wait_send()
        down_copy(g, g).wait_recv()
    local_down.wait()
    pltpu.make_async_remote_copy(
        src_ref=full_ref.at[gi], dst_ref=full_ref.at[gi], send_sem=n_send.at[1],
        recv_sem=lo_recv.at[0], device_id=(hi, me), device_id_type=MESH,
    ).wait_send()
    pltpu.make_async_remote_copy(
        src_ref=full_ref.at[gi], dst_ref=full_ref.at[gi], send_sem=n_send.at[0],
        recv_sem=hi_recv.at[0], device_id=(lo, me), device_id_type=MESH,
    ).wait_send()
    pltpu.make_async_remote_copy(
        src_ref=full_ref.at[lo, :, :, first], dst_ref=full_ref.at[lo, :, :, first],
        send_sem=r_send.at[1], recv_sem=r_recv.at[0], device_id=(hi, me), device_id_type=MESH,
    ).wait_send()
    pltpu.make_async_remote_copy(
        src_ref=full_ref.at[hi, :, :, second], dst_ref=full_ref.at[hi, :, :, second],
        send_sem=r_send.at[0], recv_sem=r_recv.at[1], device_id=(lo, me), device_id_type=MESH,
    ).wait_send()
    pltpu.make_async_remote_copy(
        src_ref=full_ref.at[far, :, :, first], dst_ref=full_ref.at[far, :, :, first],
        send_sem=r_send.at[1], recv_sem=r_recv.at[0], device_id=(hi, me), device_id_type=MESH,
    ).wait_recv()
    pltpu.make_async_remote_copy(
        src_ref=full_ref.at[far, :, :, second], dst_ref=full_ref.at[far, :, :, second],
        send_sem=r_send.at[0], recv_sem=r_recv.at[1], device_id=(lo, me), device_id_type=MESH,
    ).wait_recv()


def dispatch(send, down):
    n_exp = lax.axis_size("expert")
    n_dp = lax.axis_size("dp")
    q = down.shape[-1] // n_dp
    any_spec = pl.BlockSpec(memory_space=pl.ANY)
    moved = send.size * send.dtype.itemsize * n_dp + down.size * down.dtype.itemsize
    return pl.pallas_call(
        functools.partial(dispatch_kernel, n_exp, n_dp),
        out_shape=(
            jax.ShapeDtypeStruct((n_dp,) + send.shape, send.dtype),
            jax.ShapeDtypeStruct((n_dp,) + down.shape[:-1] + (q,), down.dtype),
        ),
        in_specs=[any_spec, any_spec],
        out_specs=(any_spec, any_spec),
        scratch_shapes=[
            pltpu.SemaphoreType.DMA((n_exp,)),
            pltpu.SemaphoreType.DMA((n_exp,)),
            pltpu.SemaphoreType.DMA((n_dp,)),
            pltpu.SemaphoreType.DMA((n_dp,)),
            pltpu.SemaphoreType.DMA((2,)),
            pltpu.SemaphoreType.DMA((n_exp,)),
            pltpu.SemaphoreType.DMA((n_exp,)),
            pltpu.SemaphoreType.DMA((2,)),
            pltpu.SemaphoreType.DMA((2,)),
            pltpu.SemaphoreType.DMA((2,)),
        ],
        compiler_params=pltpu.CompilerParams(collective_id=2, has_side_effects=True),
        cost_estimate=pl.CostEstimate(flops=0, transcendentals=0, bytes_accessed=2 * moved),
    )(send, down)


def gather_kernel(n_dp, src_ref, out_ref, send_sem, recv_sem, local_sem):
    me = lax.axis_index("expert")
    gi = lax.axis_index("dp")

    def copy_to(g, recv_slot):
        return pltpu.make_async_remote_copy(
            src_ref=src_ref,
            dst_ref=out_ref.at[recv_slot],
            send_sem=send_sem.at[g],
            recv_sem=recv_sem.at[recv_slot],
            device_id=(g, me),
            device_id_type=MESH,
        )

    barrier = pltpu.get_barrier_semaphore()
    for k in range(1, n_dp):
        pl.semaphore_signal(barrier, 1, device_id=(lax.rem(gi + k, n_dp), me), device_id_type=MESH)
    pl.semaphore_wait(barrier, n_dp - 1)
    for k in range(1, n_dp):
        copy_to(lax.rem(gi + k, n_dp), gi).start()
    local = pltpu.make_async_copy(src_ref, out_ref.at[gi], local_sem.at[0])
    local.start()
    for k in range(1, n_dp):
        g = lax.rem(gi + k, n_dp)
        copy_to(g, gi).wait_send()
        copy_to(g, g).wait_recv()
    local.wait()


def gather_dp(src):
    n_dp = lax.axis_size("dp")
    any_spec = pl.BlockSpec(memory_space=pl.ANY)
    moved = src.size * src.dtype.itemsize * n_dp
    return pl.pallas_call(
        functools.partial(gather_kernel, n_dp),
        out_shape=jax.ShapeDtypeStruct((n_dp,) + src.shape, src.dtype),
        in_specs=[any_spec],
        out_specs=any_spec,
        scratch_shapes=[
            pltpu.SemaphoreType.DMA((n_dp,)),
            pltpu.SemaphoreType.DMA((n_dp,)),
            pltpu.SemaphoreType.DMA((1,)),
        ],
        compiler_params=pltpu.CompilerParams(collective_id=3, has_side_effects=True),
        cost_estimate=pl.CostEstimate(flops=0, transcendentals=0, bytes_accessed=2 * moved),
    )(src)


def assign_slots(experts, replica_key, slot_expert):
    flat_experts = experts.reshape(-1)
    holders = (flat_experts[:, None] == slot_expert[None, :]).astype(jnp.int32)
    copies = jnp.sum(holders, axis=1)
    earlier = jnp.cumsum(holders, axis=1) - holders
    wanted = replica_key.reshape(-1) % copies
    matched = holders * (earlier == wanted[:, None]).astype(jnp.int32)
    numbers = jnp.arange(slot_expert.shape[0], dtype=jnp.int32)
    return jnp.sum(matched * numbers[None, :], axis=1)


def slot_activated(quarters, gate_up_one):
    group_count, _, quarter = quarters.shape
    unit_count = gate_up_one.shape[2]
    gate_up_out = lax.dot_general(
        quarters,
        gate_up_one.reshape(group_count, quarter, 2 * unit_count),
        (((0, 2), (0, 1)), ((), ())),
        preferred_element_type=jnp.float32,
    )
    return (jax.nn.silu(gate_up_out[:, :unit_count]) * gate_up_out[:, unit_count:]).astype(
        jnp.bfloat16
    )


def group_sums(act_all, down_cols, unit_count):
    total = None
    for group in range(act_all.shape[0]):
        lower = group * unit_count
        piece = jnp.dot(
            act_all[group],
            down_cols[lower:lower + unit_count],
            preferred_element_type=jnp.float32,
        )
        piece = piece.astype(jnp.bfloat16).astype(jnp.float32)
        total = piece if total is None else total + piece
    return total


def on_device(
    tokens,
    norm_gain,
    routing_projection_matrix,
    experts,
    replica_key,
    slot_expert,
    capacity,
    slot_gate_up_weight,
    down_weight,
):
    peer_count = lax.axis_size("expert")
    group_count = lax.axis_size("dp")
    group_pos = lax.axis_index("dp")
    me = lax.axis_index("expert")
    rows_here = tokens.shape[0]
    model_width = tokens.shape[1]
    pick_count = experts.shape[1]
    slot_count = slot_expert.shape[0]
    per_device = slot_count // peer_count
    quarter = model_width // group_count
    buffer_rows = CAP_DEV

    hidden = tokens.astype(jnp.float32)
    scale = lax.rsqrt(jnp.mean(hidden * hidden, axis=-1, keepdims=True) + 1e-06)
    normed = (hidden * scale * norm_gain.astype(jnp.float32)).astype(jnp.bfloat16)
    logits = jnp.dot(normed, routing_projection_matrix, preferred_element_type=jnp.float32)
    expert_ids = jnp.arange(logits.shape[1], dtype=jnp.int32)
    chosen = jnp.where(experts[:, :, None] == expert_ids[None, None, :], logits[:, None, :], 0.0)
    score = jax.nn.sigmoid(jnp.sum(chosen, axis=2)).reshape(-1)

    slot_ids = assign_slots(experts, replica_key, slot_expert)
    onehot = (slot_ids[:, None] == jnp.arange(slot_count, dtype=jnp.int32)[None, :]).astype(
        jnp.int32
    )
    position = jnp.sum((jnp.cumsum(onehot, axis=0) - onehot) * onehot, axis=1)
    slot_cap = jnp.sum(onehot * capacity[None, :], axis=1)
    kept_mask = position < slot_cap
    is_second = (slot_ids % per_device) == 1
    row_in = jnp.where(is_second, buffer_rows - slot_cap + position, position)
    target = jnp.where(
        kept_mask, slot_ids // per_device * buffer_rows + row_in, peer_count * buffer_rows
    )

    normed_part = lax.dynamic_slice_in_dim(normed, group_pos * quarter, quarter, 1)
    buffer_ids = jnp.arange(peer_count * buffer_rows, dtype=jnp.int32)
    hits = target.reshape(rows_here, pick_count)[None, :, :] == buffer_ids[:, None, None]
    placement = jnp.any(hits, axis=2).astype(jnp.bfloat16)
    outgoing = jnp.dot(placement, normed_part, preferred_element_type=jnp.float32)
    outgoing = outgoing.astype(jnp.bfloat16).reshape(peer_count, buffer_rows, quarter)
    full_in, down_parts = dispatch(outgoing, down_weight)
    quarters = full_in.reshape(group_count, peer_count * buffer_rows, quarter)

    first_act = slot_activated(quarters, slot_gate_up_weight[0])
    second_act = slot_activated(quarters, slot_gate_up_weight[1])
    first_cap = lax.dynamic_index_in_dim(capacity, me * per_device, keepdims=False)
    row_index = jnp.arange(peer_count * buffer_rows, dtype=jnp.int32) % buffer_rows
    in_first = (row_index < first_cap)[:, None]
    act_here = jnp.where(in_first, first_act, second_act)
    act_all = gather_dp(act_here)
    down_here = jnp.swapaxes(down_parts, 0, 1).reshape(per_device, -1, quarter)
    unit_count = down_weight.shape[1]
    first_sum = group_sums(act_all, down_here[0], unit_count)
    second_sum = group_sums(act_all, down_here[1], unit_count)
    expert_out = jnp.where(in_first, first_sum, second_sum).astype(jnp.bfloat16)
    summed = expert_out.reshape(peer_count, buffer_rows, quarter)
    (returned,) = exchange(summed, collective_id=1)

    flat_ret = returned.reshape(peer_count * buffer_rows, quarter)
    flat_ret = jnp.concatenate([flat_ret, jnp.zeros((1, quarter), flat_ret.dtype)])
    weight_kept = jnp.where(kept_mask, score, jnp.float32(0.0))
    gathered = flat_ret[target].astype(jnp.float32).reshape(rows_here, pick_count, quarter)
    mixture = jnp.sum(weight_kept.reshape(rows_here, pick_count)[:, :, None] * gathered, axis=1)
    residual = lax.dynamic_slice_in_dim(tokens, group_pos * quarter, quarter, 1).astype(jnp.float32)
    return (residual + mixture).astype(jnp.bfloat16)


def solution(mesh):
    in_specs = (
        P("expert", None),
        P(),
        P(),
        P("expert", None),
        P("expert", None),
        P(),
        P(),
        P("expert", None, None, "dp"),
        P("expert", "dp", None),
    )
    out_specs = P("expert", "dp")
    return jax.shard_map(
        on_device, mesh=mesh, in_specs=in_specs, out_specs=out_specs, check_vma=False
    )
```
